128 devices in a mesh: row: 4 (over y), col: 32 (over z, x, core).
Axes of the slice: x: 4, y: 4, z: 4, core: 2. Of those that a mesh axis runs over, the one named last changes fastest.
Arguments:
- rhs: float32 [16384, 256], P(('row', 'col')), may hold values from -6 to 6
- dense: float32 [2, 16384, 16384], P(None, 'col', 'row'), may hold values from -0.03125 to 0.03125
- inflow: float32 [128, 2, 2, 512, 256], P(('row', 'col')), may hold values from -0.25 to 0.25
- robin: float32 [128, 2, 2, 512, 512], P(('row', 'col')), may hold values from -0.1875 to 0.1875
- outflow: float32 [128, 2, 256, 1024], P(('row', 'col')), may hold values from -0.0390625 to 0.0390625
- trace_row: int32 [32, 128, 8], replicated, may hold values from 0 to 511
- trace_count: int32 [32, 128], replicated, may hold values from 0 to 8, as said below
- current_row: int32 [128, 128, 2], replicated, may hold values from 0 to 127
- current_count: int32 [128, 128], replicated, may hold values from 0 to 2, as said below
Outputs:
- solution: float32 [16384, 256], P(('row', 'col'))
The draws below stay inside these ranges and needn't reach their ends.
Inputs may be any that keep to these rules, and one draw needn't show every extreme that they name: `trace_row`: repeats may occur. `trace_count`: 8 is reached, and some subdomain takes 8 from every block. `current_row`: repeats may occur. `current_count`: some subdomain gives 2 to every block, and some block receives 2 from every subdomain.
All inputs are finite; a program needn't handle non-finite values.
Results may differ from the reference program's by a relative error of at most 0.0001.
Values sent between devices are 32-bit elements; how exact they have to be, the bound alone decides.
A program may use at most 128 MiB of HBM per device.

```python
import jax
import jax.numpy as jnp
from jax import lax

NS = 16384
M = 512
W = 128
TPAIR = 8
TB = 2
ITERS = 2
SUBS = 128
COLS = 32
GROUP = 512
SB = 128
CAP = 256
CAPB = 256


def draw_trace_count(key, part):
    first, second, third = jax.random.split(jax.random.fold_in(key, 11), 3)
    level = jax.random.randint(first, (SUBS,), 0, TPAIR + 1)
    drawn = jax.random.randint(second, (COLS, SUBS), 0, 2 * TPAIR + 1)
    counts = jnp.minimum(TPAIR, drawn * level[None, :] // TPAIR)
    chosen = jax.random.randint(third, (), 0, SUBS)
    column = jnp.arange(SUBS)[None, :]
    return jnp.where(column == chosen, TPAIR, counts).astype(jnp.int32)


def draw_current_count(key, part):
    first, second, third, fourth = jax.random.split(jax.random.fold_in(key, 23), 4)
    level = jax.random.randint(first, (SUBS,), 0, TB + 1)
    drawn = jax.random.randint(second, (SUBS, SUBS), 0, 2 * TB + 1)
    counts = jnp.minimum(TB, drawn * level[None, :] // TB)
    sender = jax.random.randint(third, (), 0, SUBS)
    receiver = jax.random.randint(fourth, (), 0, SUBS)
    column = jnp.arange(SUBS)[None, :]
    line = jnp.arange(SUBS)[:, None]
    counts = jnp.where(column == sender, TB, counts)
    counts = jnp.where(line == receiver, TB, counts)
    return counts.astype(jnp.int32)


def plant(array, own_key, low, top_value):
    shape = array.shape
    index_at = [jax.random.randint(jax.random.fold_in(own_key, axis), (), 0, shape[axis]) for axis in range(len(shape))]
    array = array.at[tuple(index_at)].set(low)
    longest = shape.index(max(shape))
    index_at[longest] = (index_at[longest] + 1) % shape[longest]
    return array.at[tuple(index_at)].set(top_value)


def levels(stream_key, extent, cuts, low, high):
    gain = 1.0
    for axis_at, shards_of in cuts:
        draws = jax.random.uniform(jax.random.fold_in(jax.random.fold_in(stream_key, 6), axis_at), (shards_of,), jnp.float32, low / len(cuts), high / len(cuts))
        gain = gain * jnp.repeat(jnp.exp(draws), extent[axis_at] // shards_of).reshape((-1,) + (1,) * (len(extent) - 1 - axis_at))
    return gain


def centred(own_key, extent, deviation, limit, pieces=(), kind=jnp.bfloat16):
    values = jax.random.normal(own_key, extent, jnp.float32) * deviation
    if len(pieces) > 0:
        values = levels(own_key, extent, pieces, -0.22, 0.18) * values
    return jnp.clip(values, min=-limit, max=limit).astype(kind)


def setup_inputs(seed: int = 0) -> dict:
    key_list = jax.random.split(jax.random.key(seed), 10)
    return {
        "rhs": centred(key_list[0], (NS, 2 * W), 1.0, 6.0, ((0, 128),), jnp.float32),
        "dense": centred(key_list[1], (2, NS, NS), (2 * NS) ** -0.5, 0.03125, ((1, 32), (2, 4)), jnp.float32),
        "inflow": centred(key_list[2], (SUBS, 2, 2, M, CAP), (2 * CAP) ** -0.5, 0.25, ((0, 128),), jnp.float32),
        "robin": centred(key_list[3], (SUBS, 2, 2, M, M), (2 * M) ** -0.5, 0.1875, ((0, 128),), jnp.float32),
        "outflow": centred(key_list[4], (SUBS, 2, CAPB, 2 * M), (48 * M) ** -0.5, 0.0390625, ((0, 128),), jnp.float32),
        "trace_row": plant(jax.random.randint(key_list[5], (COLS, SUBS, TPAIR), 0, GROUP), jax.random.fold_in(key_list[5], 1), 0, GROUP - 1).astype(jnp.int32),
        "trace_count": draw_trace_count(jax.random.fold_in(key_list[9], 71), 0),
        "current_row": plant(jax.random.randint(key_list[7], (SUBS, SUBS, TB), 0, SB), jax.random.fold_in(key_list[7], 1), 0, SB - 1).astype(jnp.int32),
        "current_count": draw_current_count(jax.random.fold_in(key_list[9], 71), 0),
    }


EPS = 1e-06
HIGH = lax.Precision.HIGHEST

def combine(real_half, imag_half, waves):
    return jnp.concatenate([real_half[..., :waves] - imag_half[..., waves:], real_half[..., waves:] + imag_half[..., :waves]], axis=-1)

def scale_vector(vector, coef, waves):
    real_part = vector[:, :waves]
    imag_part = vector[:, waves:]
    return jnp.concatenate([coef[0] * real_part - coef[1] * imag_part, coef[0] * imag_part + coef[1] * real_part], axis=1)

def inner_terms(left, right, waves):
    left_real, left_imag = (left[:, :waves], left[:, waves:])
    right_real, right_imag = (right[:, :waves], right[:, waves:])
    return (lax.optimization_barrier(jnp.sum(left_real * right_real + left_imag * right_imag, axis=0)), lax.optimization_barrier(jnp.sum(left_real * right_imag - left_imag * right_real, axis=0)))

def square_terms(vector, waves):
    halves = lax.optimization_barrier(jnp.sum(vector * vector, axis=0))
    return halves[:waves] + halves[waves:]

def cmul(first, second):
    return (first[0] * second[0] - first[1] * second[1], first[0] * second[1] + first[1] * second[0])

def cconj(first):
    return (first[0], -first[1])

def csub(first, second):
    return (first[0] - second[0], first[1] - second[1])

def cadd(first, second):
    return (first[0] + second[0], first[1] + second[1])

def cdiv(first, second):
    denom = second[0] * second[0] + second[1] * second[1]
    numer = cmul(first, cconj(second))
    return (numer[0] / denom, numer[1] / denom)

def solve_small(gram, target):
    size = len(target)
    gram = [list(line) for line in gram]
    target = list(target)
    for pivot in range(size):
        for lower in range(pivot + 1, size):
            factor = cdiv(gram[lower][pivot], gram[pivot][pivot])
            for other in range(pivot, size):
                gram[lower][other] = csub(gram[lower][other], cmul(factor, gram[pivot][other]))
            target[lower] = csub(target[lower], cmul(factor, target[pivot]))
    result = [None] * size
    for pivot in reversed(range(size)):
        summed = target[pivot]
        for other in range(pivot + 1, size):
            summed = csub(summed, cmul(gram[pivot][other], result[other]))
        result[pivot] = cdiv(summed, gram[pivot][pivot])
    return result

def least_squares(hess, beta, steps):
    zero_pair = (jnp.zeros_like(beta), jnp.zeros_like(beta))
    gram = []
    for first in range(steps):
        line = []
        for second in range(steps):
            summed = zero_pair
            for height in range(steps + 1):
                summed = cadd(summed, cmul(cconj(hess.get((height, first), zero_pair)), hess.get((height, second), zero_pair)))
            line.append(summed)
        gram.append(line)
    target = [cmul(cconj(hess.get((0, first), zero_pair)), (beta, jnp.zeros_like(beta))) for first in range(steps)]
    return solve_small(gram, target)

def reference(rhs, dense, inflow, robin, outflow, trace_row, trace_count, current_row, current_count):
    waves = rhs.shape[1] // 2
    lanes = rhs.shape[1]

    def operate(vector):
        real_half = jnp.dot(dense[0], vector, precision=HIGH, preferred_element_type=jnp.float32)
        imag_half = jnp.dot(dense[1], vector, precision=HIGH, preferred_element_type=jnp.float32)
        field = combine(real_half, imag_half, waves)
        rows = jnp.arange(COLS, dtype=jnp.int32)[:, None, None] * GROUP + trace_row
        keep = (jnp.arange(TPAIR, dtype=jnp.int32)[None, None, :] < trace_count[:, :, None]).astype(jnp.float32)
        slots = field[rows.reshape(-1)].reshape(COLS, SUBS, TPAIR, lanes) * keep[..., None]
        slots = jnp.transpose(slots, (1, 0, 2, 3)).reshape(SUBS, CAP, lanes)
        mixed = jnp.einsum('dfpmk,dkl->dfpml', inflow, slots, precision=HIGH)
        excite = combine(mixed[:, :, 0], mixed[:, :, 1], waves)
        mixed = jnp.einsum('dfpmn,dfnl->dfpml', robin, excite, precision=HIGH)
        local = combine(mixed[:, :, 0], mixed[:, :, 1], waves)
        empty = jnp.zeros((1, M, lanes), jnp.float32)
        left_side = jnp.concatenate([empty, local[:-1, 1]], axis=0)
        right_side = jnp.concatenate([local[1:, 0], empty], axis=0)
        near = jnp.stack([left_side, right_side], axis=1)
        mixed = jnp.einsum('dfpmn,dfnl->dfpml', robin, near, precision=HIGH)
        faces = local + combine(mixed[:, :, 0], mixed[:, :, 1], waves)
        flat = faces.reshape(SUBS, 2 * M, lanes)
        mixed = jnp.einsum('dpkn,dnl->dpkl', outflow, flat, precision=HIGH)
        currents = combine(mixed[:, 0], mixed[:, 1], waves).reshape(SUBS, SUBS, TB, lanes)
        targets = jnp.arange(SUBS, dtype=jnp.int32)[:, None, None] * SB + current_row
        alive = (jnp.arange(TB, dtype=jnp.int32)[None, None, :] < current_count[:, :, None]).astype(jnp.float32)
        values = jnp.transpose(currents, (1, 0, 2, 3)) * alive[..., None]
        back = jnp.zeros((NS, lanes), jnp.float32).at[targets.reshape(-1)].add(values.reshape(-1, lanes))
        return vector + back
    beta = jnp.sqrt(square_terms(rhs, waves) + EPS)
    basis = [rhs / jnp.concatenate([beta, beta])[None, :]]
    hess = {}
    for step in range(ITERS):
        image = operate(basis[step])
        remain = square_terms(image, waves)
        for column in range(step + 1):
            coef = inner_terms(basis[column], image, waves)
            hess[column, step] = coef
            remain = remain - coef[0] * coef[0] - coef[1] * coef[1]
        height = jnp.sqrt(remain + EPS)
        hess[step + 1, step] = (height, jnp.zeros_like(height))
        if step + 1 < ITERS:
            update = image
            for column in range(step + 1):
                update = update - scale_vector(basis[column], hess[column, step], waves)
            basis.append(update / jnp.concatenate([height, height])[None, :])
    coeffs = least_squares(hess, beta, ITERS)
    solution = jnp.zeros_like(rhs)
    for column in range(ITERS):
        solution = solution + scale_vector(basis[column], coeffs[column], waves)
    return solution
```

```python
import jax
import jax.numpy as jnp
from jax import lax
from jax.sharding import PartitionSpec as P

ITERS = 2


EPS = 1e-06
SCALE = 2.0**-24
HIGH = lax.Precision.HIGH


def extended(x, sides, width):
    for axis, dim in sides:
        size, length = (lax.axis_size(axis), x.shape[dim])
        up = [(i, (i + 1) % size) for i in range(size - 1)]
        down = [(j, i) for i, j in up]
        last = lax.slice_in_dim(x, length - width, length, axis=dim)
        leading = lax.slice_in_dim(x, 0, width, axis=dim)
        before = lax.ppermute(last, axis, up)
        after = lax.ppermute(leading, axis, down)
        x = jnp.concatenate([before, x, after], axis=dim)
    return x


def combine(real_half, imag_half, waves):
    return jnp.concatenate(
        [
            real_half[..., :waves] - imag_half[..., waves:],
            real_half[..., waves:] + imag_half[..., :waves],
        ],
        axis=-1,
    )


def scale_vector(vector, coef, waves):
    real_part = vector[:, :waves]
    imag_part = vector[:, waves:]
    return jnp.concatenate(
        [coef[0] * real_part - coef[1] * imag_part, coef[0] * imag_part + coef[1] * real_part],
        axis=1,
    )


def inner_terms(left, right, waves):
    left_real, left_imag = (left[:, :waves], left[:, waves:])
    right_real, right_imag = (right[:, :waves], right[:, waves:])
    return (
        jnp.sum(left_real * right_real + left_imag * right_imag, axis=0),
        jnp.sum(left_real * right_imag - left_imag * right_real, axis=0),
    )


def square_terms(vector, waves):
    halves = jnp.sum(vector * vector, axis=0)
    return halves[:waves] + halves[waves:]


def cmul(first, second):
    return (
        first[0] * second[0] - first[1] * second[1],
        first[0] * second[1] + first[1] * second[0],
    )


def cconj(first):
    return (first[0], -first[1])


def csub(first, second):
    return (first[0] - second[0], first[1] - second[1])


def cadd(first, second):
    return (first[0] + second[0], first[1] + second[1])


def cdiv(first, second):
    denom = second[0] * second[0] + second[1] * second[1]
    numer = cmul(first, cconj(second))
    return (numer[0] / denom, numer[1] / denom)


def solve_small(gram, target):
    size = len(target)
    gram = [list(line) for line in gram]
    target = list(target)
    for pivot in range(size):
        for lower in range(pivot + 1, size):
            factor = cdiv(gram[lower][pivot], gram[pivot][pivot])
            for other in range(pivot, size):
                gram[lower][other] = csub(gram[lower][other], cmul(factor, gram[pivot][other]))
            target[lower] = csub(target[lower], cmul(factor, target[pivot]))
    result = [None] * size
    for pivot in reversed(range(size)):
        summed = target[pivot]
        for other in range(pivot + 1, size):
            summed = csub(summed, cmul(gram[pivot][other], result[other]))
        result[pivot] = cdiv(summed, gram[pivot][pivot])
    return result


def least_squares(hess, beta, steps):
    zero_pair = (jnp.zeros_like(beta), jnp.zeros_like(beta))
    gram = []
    for first in range(steps):
        line = []
        for second in range(steps):
            summed = zero_pair
            for height in range(steps + 1):
                summed = cadd(
                    summed,
                    cmul(
                        cconj(hess.get((height, first), zero_pair)),
                        hess.get((height, second), zero_pair),
                    ),
                )
            line.append(summed)
        gram.append(line)
    target = [
        cmul(cconj(hess.get((0, first), zero_pair)), (beta, jnp.zeros_like(beta)))
        for first in range(steps)
    ]
    return solve_small(gram, target)


def turned(vector, waves):
    return jnp.concatenate([-vector[..., waves:], vector[..., :waves]], axis=-1)


def conj_mul(first, second):
    return cmul(cconj(first), second)


def krylov_coefficients(sums):
    norm0, p_real, p_imag, norm1, t_real, t_imag, s_real, s_imag, norm2 = sums
    zero = jnp.zeros_like(norm0)
    beta2 = norm0 + EPS
    beta = jnp.sqrt(beta2)
    unit = norm0 / beta2
    lack = EPS / beta2
    p = (p_real / beta2, p_imag / beta2)
    q = norm1 / beta2
    back = 1.0 / SCALE
    t = ((t_real / beta2) * back, (t_imag / beta2) * back)
    s = ((s_real / beta2) * back, (s_imag / beta2) * back)
    z = ((norm2 / beta2) * back) * back
    p_abs = p[0] * p[0] + p[1] * p[1]
    h00 = (unit + p[0], p[1])
    h10 = jnp.sqrt(unit * lack + 2.0 * lack * p[0] + (q - p_abs) + EPS)
    a = 1.0 / h10
    g = (lack - p[0], -p[1])
    g_abs = g[0] * g[0] + g[1] * g[1]
    gp = cmul(g, p)
    h01 = (
        a * (lack * h00[0] + (t[0] + gp[0])),
        a * (lack * h00[1] + (t[1] + gp[1])),
    )
    short = a * a * (lack * (1.0 - lack) * (unit + 2.0 * p[0]) + lack * p_abs + EPS)
    length = 1.0 - short
    gt = conj_mul(g, t)
    m = (
        a * a * (s[0] + g[0] * q + gt[0] + g_abs * p[0]),
        a * a * (s[1] + g[1] * q + gt[1] + g_abs * p[1]),
    )
    spread = a * a * (z + 2.0 * conj_mul(g, s)[0] + g_abs * q)
    h11 = (length + m[0], m[1])
    remain = length * short + 2.0 * short * m[0] + (spread - m[0] * m[0] - m[1] * m[1])
    remain = remain - h01[0] * h01[0] - h01[1] * h01[1]
    h21 = jnp.sqrt(remain + EPS)
    hess = {(0, 0): h00, (1, 0): (h10, zero), (0, 1): h01, (1, 1): h11, (2, 1): (h21, zero)}
    y0, y1 = least_squares(hess, beta, ITERS)
    ya = (y1[0] * a, y1[1] * a)
    yg = cmul(ya, g)
    return ((y0[0] + yg[0]) / beta, (y0[1] + yg[1]) / beta), (ya[0] / beta, ya[1] / beta)


def on_device(
    rhs, dense, inflow, robin, outflow, trace_row, trace_count, current_row, current_count
):
    n_row = lax.axis_size("row")
    n_col = lax.axis_size("col")
    devices = n_row * n_col
    row_at = lax.axis_index("row")
    col_at = lax.axis_index("col")
    device_at = row_at * n_col + col_at
    block_rows, lanes = rhs.shape
    waves = lanes // 2
    tpair = trace_row.shape[2]
    tback = current_row.shape[2]
    inflow_mine = inflow[0]
    robin_mine = robin[0]
    outflow_mine = outflow[0]
    trace_rows = lax.dynamic_index_in_dim(trace_row, col_at, 0, keepdims=False)
    trace_live = lax.dynamic_index_in_dim(trace_count, col_at, 0, keepdims=False)
    trace_keep = (jnp.arange(tpair, dtype=jnp.int32)[None, :] < trace_live[:, None]).astype(
        jnp.float32
    )

    basis = [rhs]
    for step in range(ITERS):
        operate_vector = basis[step] if step == 0 else basis[step] * SCALE
        piece = lax.all_gather(operate_vector, "col", axis=0, tiled=True)
        real_cols = dense[0]
        imag_cols = dense[1]
        field = jnp.dot(real_cols, piece, precision=HIGH, preferred_element_type=jnp.float32)
        field = field + jnp.dot(
            imag_cols, turned(piece, waves), precision=HIGH, preferred_element_type=jnp.float32
        )
        buffer = (
            jnp.take(field, trace_rows.reshape(-1), axis=0).reshape(
                devices, tpair, lanes
            )
            * trace_keep[:, :, None]
        )
        arrived = lax.all_to_all(buffer, ("row", "col"), split_axis=0, concat_axis=0, tiled=True)
        slots = jnp.sum(arrived.reshape(n_row, n_col, tpair, lanes), axis=0)
        slots = slots.reshape(n_col * tpair, lanes)
        mixed = jnp.einsum("fpmk,kl->fpml", inflow_mine, slots, precision=HIGH)
        excite = combine(mixed[:, 0], mixed[:, 1], waves)
        mixed = jnp.einsum("fpmn,fnl->fpml", robin_mine, excite, precision=HIGH)
        local = combine(mixed[:, 0], mixed[:, 1], waves)
        padded = extended(local, ((("row", "col"), 0),), 1)
        near = jnp.stack([padded[0], padded[3]], axis=0)
        mixed = jnp.einsum("fpmn,fnl->fpml", robin_mine, near, precision=HIGH)
        faces = local + combine(mixed[:, 0], mixed[:, 1], waves)
        flat = faces.reshape(faces.shape[0] * faces.shape[1], lanes)
        mixed = jnp.einsum("pkn,nl->pkl", outflow_mine, flat, precision=HIGH)
        currents = combine(mixed[0], mixed[1], waves)
        operate_arrived = lax.all_to_all(
            currents.reshape(devices, tback, lanes),
            ("row", "col"),
            split_axis=0,
            concat_axis=0,
            tiled=True,
        )
        own_rows = lax.dynamic_index_in_dim(current_row, device_at, 0, keepdims=False)
        own_live = lax.dynamic_index_in_dim(current_count, device_at, 0, keepdims=False)
        alive = (jnp.arange(tback, dtype=jnp.int32)[None, :] < own_live[:, None]).astype(
            jnp.float32
        )
        landed = (
            jnp.zeros((block_rows, lanes), jnp.float32)
            .at[own_rows.reshape(-1)]
            .add((operate_arrived * alive[..., None]).reshape(-1, lanes))
        )
        basis.append(landed)
    u0, b0, b1 = basis
    sums = [square_terms(u0, waves), *inner_terms(u0, b0, waves), square_terms(b0, waves)]
    sums += [*inner_terms(u0, b1, waves), *inner_terms(b0, b1, waves), square_terms(b1, waves)]
    sums = lax.psum(jnp.stack(sums, axis=0), ("row", "col"))
    first, second = krylov_coefficients([sums[i] for i in range(9)])
    return scale_vector(u0, first, waves) + scale_vector(b0, second, waves)


def solution(mesh):
    placed = (
        P(("row", "col"), None),
        P(None, "col", "row"),
        P(("row", "col"), None, None, None, None),
        P(("row", "col"), None, None, None, None),
        P(("row", "col"), None, None, None),
        P(),
        P(),
        P(),
        P(),
    )
    return jax.shard_map(
        on_device, mesh=mesh, in_specs=placed, out_specs=P(("row", "col"), None), check_vma=False
    )
```

```python
import functools

import jax
import jax.numpy as jnp
from jax import lax
from jax.experimental import pallas as pl
from jax.experimental.pallas import tpu as pltpu
from jax.sharding import PartitionSpec as P

ITERS = 2


EPS = 1e-06
SCALE = 2.0**-24
MESH = pl.DeviceIdType.MESH


def scale_vector(vector, coef, waves):
    real_part = vector[:, :waves]
    imag_part = vector[:, waves:]
    return jnp.concatenate(
        [coef[0] * real_part - coef[1] * imag_part, coef[0] * imag_part + coef[1] * real_part],
        axis=1,
    )


def inner_terms(left, right, waves):
    left_real, left_imag = (left[:, :waves], left[:, waves:])
    right_real, right_imag = (right[:, :waves], right[:, waves:])
    return (
        jnp.sum(left_real * right_real + left_imag * right_imag, axis=0),
        jnp.sum(left_real * right_imag - left_imag * right_real, axis=0),
    )


def square_terms(vector, waves):
    halves = jnp.sum(vector * vector, axis=0)
    return halves[:waves] + halves[waves:]


def cmul(first, second):
    return (
        first[0] * second[0] - first[1] * second[1],
        first[0] * second[1] + first[1] * second[0],
    )


def cconj(first):
    return (first[0], -first[1])


def csub(first, second):
    return (first[0] - second[0], first[1] - second[1])


def cadd(first, second):
    return (first[0] + second[0], first[1] + second[1])


def cdiv(first, second):
    denom = second[0] * second[0] + second[1] * second[1]
    numer = cmul(first, cconj(second))
    return (numer[0] / denom, numer[1] / denom)


def solve_small(gram, target):
    size = len(target)
    gram = [list(line) for line in gram]
    target = list(target)
    for pivot in range(size):
        for lower in range(pivot + 1, size):
            factor = cdiv(gram[lower][pivot], gram[pivot][pivot])
            for other in range(pivot, size):
                gram[lower][other] = csub(gram[lower][other], cmul(factor, gram[pivot][other]))
            target[lower] = csub(target[lower], cmul(factor, target[pivot]))
    result = [None] * size
    for pivot in reversed(range(size)):
        summed = target[pivot]
        for other in range(pivot + 1, size):
            summed = csub(summed, cmul(gram[pivot][other], result[other]))
        result[pivot] = cdiv(summed, gram[pivot][pivot])
    return result


def least_squares(hess, beta, steps):
    zero_pair = (jnp.zeros_like(beta), jnp.zeros_like(beta))
    gram = []
    for first in range(steps):
        line = []
        for second in range(steps):
            summed = zero_pair
            for height in range(steps + 1):
                summed = cadd(
                    summed,
                    cmul(
                        cconj(hess.get((height, first), zero_pair)),
                        hess.get((height, second), zero_pair),
                    ),
                )
            line.append(summed)
        gram.append(line)
    target = [
        cmul(cconj(hess.get((0, first), zero_pair)), (beta, jnp.zeros_like(beta)))
        for first in range(steps)
    ]
    return solve_small(gram, target)


def turned(vector):
    waves = vector.shape[-1] // 2
    return jnp.concatenate([-vector[..., waves:], vector[..., :waves]], axis=-1)


def conj_mul(first, second):
    return cmul(cconj(first), second)


def krylov_coefficients(sums):
    norm0, p_real, p_imag, norm1, t_real, t_imag, s_real, s_imag, norm2 = sums
    zero = jnp.zeros_like(norm0)
    beta2 = norm0 + EPS
    beta = jnp.sqrt(beta2)
    unit = norm0 / beta2
    lack = EPS / beta2
    p = (p_real / beta2, p_imag / beta2)
    q = norm1 / beta2
    back = 1.0 / SCALE
    t = ((t_real / beta2) * back, (t_imag / beta2) * back)
    s = ((s_real / beta2) * back, (s_imag / beta2) * back)
    z = ((norm2 / beta2) * back) * back
    p_abs = p[0] * p[0] + p[1] * p[1]
    h00 = (unit + p[0], p[1])
    h10 = jnp.sqrt(unit * lack + 2.0 * lack * p[0] + (q - p_abs) + EPS)
    a = 1.0 / h10
    g = (lack - p[0], -p[1])
    g_abs = g[0] * g[0] + g[1] * g[1]
    gp = cmul(g, p)
    h01 = (
        a * (lack * h00[0] + (t[0] + gp[0])),
        a * (lack * h00[1] + (t[1] + gp[1])),
    )
    short = a * a * (lack * (1.0 - lack) * (unit + 2.0 * p[0]) + lack * p_abs + EPS)
    length = 1.0 - short
    gt = conj_mul(g, t)
    m = (
        a * a * (s[0] + g[0] * q + gt[0] + g_abs * p[0]),
        a * a * (s[1] + g[1] * q + gt[1] + g_abs * p[1]),
    )
    spread = a * a * (z + 2.0 * conj_mul(g, s)[0] + g_abs * q)
    h11 = (length + m[0], m[1])
    remain = length * short + 2.0 * short * m[0] + (spread - m[0] * m[0] - m[1] * m[1])
    remain = remain - h01[0] * h01[0] - h01[1] * h01[1]
    h21 = jnp.sqrt(remain + EPS)
    hess = {(0, 0): h00, (1, 0): (h10, zero), (0, 1): h01, (1, 1): h11, (2, 1): (h21, zero)}
    y0, y1 = least_squares(hess, beta, ITERS)
    ya = (y1[0] * a, y1[1] * a)
    yg = cmul(ya, g)
    return ((y0[0] + yg[0]) / beta, (y0[1] + yg[1]) / beta), (ya[0] / beta, ya[1] / beta)


def split(x):
    high = x.astype(jnp.bfloat16)
    return high, (x - high.astype(jnp.float32)).astype(jnp.bfloat16)


def mm(a, b):
    return jnp.dot(a, b, preferred_element_type=jnp.float32)


def dot3(a, b):
    a_high, a_low = split(a)
    b_high, b_low = split(b)
    return mm(a_high, b_high) + (mm(a_high, b_low) + mm(a_low, b_high))


def pick(onehot, x):
    high, low = split(x)
    return mm(onehot, high) + mm(onehot, low)


def stacked(x):
    return jnp.concatenate([x, turned(x)], axis=0)


EVENTS = [
    (0, 0), (-1, 0), (1, 0), (0, -1), (0, 1), (2, 0), (-1, -1), (-1, 1),
    (1, -1), (1, 1), (0, 2), (2, -1), (2, 1), (-1, 2), (1, 2), (2, 2),
]


def kernel(
    n_row, n_col,
    rhs_hbm, dense_hbm, inflow_hbm, robin_hbm, outflow_hbm, tid_ref, sid_ref,
    out_ref,
    vfull, dstage, acc, gmat, gbuf, ybuf, sbuf, slots, infl, rob, outf,
    rin, orob, town, faces, nbuf, cur, curh, zbuf, zz, fin, basis, gram, gy, gram2, gc,
    load_sem, dsem, ag_send, ag_recv, y_send, y_recv, c_send, c_recv,
    f_send, f_recv, z_send, z_recv, e_send, e_recv, gy_send, gy_recv, gc_send, gc_recv,
):
    row = lax.axis_index("row")
    col = lax.axis_index("col")
    device = row * n_col + col
    total = n_row * n_col
    up = lax.rem(device + 1, total)
    down = lax.rem(device + total - 1, total)
    z = col // 8
    x = lax.rem(col // 2, 4)
    core = lax.rem(col, 2)
    stride_a = 8 - 6 * core
    stride_b = 2 + 6 * core
    at_a = z * (1 - core) + x * core
    at_b = x * (1 - core) + z * core

    def mine(da, db):
        return lax.rem(at_a + (da + 4), 4) * stride_a + lax.rem(at_b + (db + 4), 4) * stride_b + core

    def theirs(da, db):
        return (
            lax.rem(at_b + (da + 4), 4) * stride_b
            + lax.rem(at_a + (db + 4), 4) * stride_a
            + (1 - core)
        )

    partner = col + 1 - 2 * core
    half_rows = vfull.shape[1] // 2

    loads = [
        pltpu.make_async_copy(rhs_hbm, vfull.at[col], load_sem.at[0]),
        pltpu.make_async_copy(rhs_hbm, basis.at[0], load_sem.at[1]),
    ]
    for copy in loads:
        copy.start()

    def dense_copy(part, index):
        return pltpu.make_async_copy(
            dense_hbm.at[part, :, pl.ds(pl.multiple_of(index * 128, 128), 128)],
            dstage.at[index, :, pl.ds(part * 128, 128)],
            dsem.at[part, index],
        )

    @pl.loop(0, n_col)
    def _(k):
        index = lax.rem(col + k, n_col)
        dense_copy(0, index).start()
        dense_copy(1, index).start()

    small = []
    for face in range(2):
        for part in range(2):
            small.append(
                pltpu.make_async_copy(
                    inflow_hbm.at[0, face, part],
                    infl.at[face, :, pl.ds(part * 256, 256)],
                    load_sem.at[2 + len(small)],
                )
            )
            small.append(
                pltpu.make_async_copy(
                    robin_hbm.at[0, face, part],
                    rob.at[face, :, pl.ds(part * 512, 512)],
                    load_sem.at[2 + len(small)],
                )
            )
            small.append(
                pltpu.make_async_copy(
                    outflow_hbm.at[0, part, :, pl.ds(face * 512, 512)],
                    outf.at[face, :, pl.ds(part * 512, 512)],
                    load_sem.at[2 + len(small)],
                )
            )
    for copy in small:
        copy.start()

    barrier = pltpu.get_barrier_semaphore()

    @pl.loop(1, n_col)
    def _(k):
        other = lax.rem(col + k, n_col)
        pl.semaphore_signal(barrier, inc=1, device_id=(row, other), device_id_type=MESH)

    for k in range(1, n_row):
        other = lax.rem(row + k, n_row)
        pl.semaphore_signal(barrier, inc=1, device_id=(other, col), device_id_type=MESH)
    for other in (up, down):
        pl.semaphore_signal(
            barrier,
            inc=1,
            device_id=(other // n_col, lax.rem(other, n_col)),
            device_id_type=MESH,
        )
    pl.semaphore_wait(barrier, n_col - 1 + n_row - 1 + 2)
    for copy in loads:
        copy.wait()

    def operate(step):
        sends = []

        def send(index, target, half=None):
            if half is None:
                ref, arrive = vfull.at[index], ag_recv.at[index, 0]
            else:
                ref = vfull.at[index, pl.ds(half * half_rows, half_rows)]
                arrive = ag_recv.at[index, half]
            copy = pltpu.make_async_remote_copy(
                src_ref=ref,
                dst_ref=ref,
                send_sem=ag_send.at[len(sends)],
                recv_sem=arrive,
                device_id=(row, target),
                device_id_type=MESH,
            )
            copy.start()
            sends.append(copy)

        def await_chunk(index, halves):
            if halves:
                for half in range(2):
                    ref = vfull.at[index, pl.ds(half * half_rows, half_rows)]
                    pltpu.make_async_remote_copy(
                        src_ref=ref, dst_ref=ref, send_sem=ag_send.at[0],
                        recv_sem=ag_recv.at[index, half],
                        device_id=(row, partner), device_id_type=MESH,
                    ).wait_recv()
            else:
                ref = vfull.at[index]
                pltpu.make_async_remote_copy(
                    src_ref=ref, dst_ref=ref, send_sem=ag_send.at[0],
                    recv_sem=ag_recv.at[index, 0],
                    device_id=(row, partner), device_id_type=MESH,
                ).wait_recv()

        def multiply(index):
            @pl.when(step == 0)
            def _():
                dense_copy(0, index).wait()
                dense_copy(1, index).wait()

            acc[...] += dot3(dstage[index], stacked(vfull[index]))

        acc[...] = jnp.zeros_like(acc)
        late = None
        for da, db in EVENTS:
            index = mine(da, db)
            if (da, db) != (0, 0):
                await_chunk(index, db == 2 or (da == 2 and db == 0))
            if db == 0:
                if da == 0:
                    send(index, mine(1, 0))
                    send(index, mine(-1, 0))
                elif da == -1:
                    send(index, mine(1, 0), 0)
                elif da == 1:
                    send(index, mine(-1, 0), 1)
                send(index, mine(0, 1))
                send(index, mine(0, -1))
            elif db == -1:
                send(index, mine(0, 1), 0)
            elif db == 1:
                send(index, mine(0, -1), 1)
            send(index, partner)
            if late is None:
                multiply(index)
            else:
                await_chunk(late, False)

                def two(j, carry, index=index, late=late):
                    multiply(index * (1 - j) + late * j)
                    return carry

                lax.fori_loop(0, 2, two, 0)
            late = theirs(da, db)
        await_chunk(late, False)
        multiply(late)
        for copy in sends:
            copy.wait_send()

        @pl.when(step == 0)
        def _():
            gmat[...] = jnp.where(
                tid_ref[...] == lax.broadcasted_iota(jnp.int32, gmat.shape, 1), 1.0, 0.0
            ).astype(jnp.bfloat16)

        def y_copy(k):
            other = lax.rem(row + k, n_row)
            return pltpu.make_async_remote_copy(
                src_ref=gbuf.at[other],
                dst_ref=ybuf.at[row],
                send_sem=y_send.at[k],
                recv_sem=y_recv.at[row],
                device_id=(other, col),
                device_id_type=MESH,
            )

        def y_wait(k):
            other = lax.rem(row + k, n_row)
            pltpu.make_async_remote_copy(
                src_ref=gbuf.at[other],
                dst_ref=ybuf.at[other],
                send_sem=y_send.at[k],
                recv_sem=y_recv.at[other],
                device_id=(other, col),
                device_id_type=MESH,
            ).wait_recv()

        def trace(k, carry):
            ahead = n_row - 1 - k
            other = lax.rem(row + ahead, n_row)
            rows = pl.ds(pl.multiple_of(other * 256, 256), 256)
            gbuf[other] = pick(gmat[rows, :], acc[...])

            @pl.when(k < 3)
            def _():
                y_copy(ahead).start()

            return carry

        lax.fori_loop(0, n_row, trace, 0)

        @pl.when(step == 0)
        def _():
            for copy in small:
                copy.wait()

            def face_maps(face, carry):
                real, imag = infl[face, :, 0:256], infl[face, :, 256:512]
                rin[face, :, 0:256] = dot3(rob[face], jnp.concatenate([real, -imag], axis=0))
                rin[face, :, 256:512] = dot3(rob[face], jnp.concatenate([imag, real], axis=0))

                for tile in range(2):
                    at = tile * 256
                    real = rob[face, :, pl.ds(at, 256)]
                    imag = rob[face, :, pl.ds(512 + at, 256)]
                    orob[face, :, pl.ds(at, 256)] = dot3(
                        outf[face], jnp.concatenate([real, -imag], axis=0)
                    )
                    orob[face, :, pl.ds(512 + at, 256)] = dot3(
                        outf[face], jnp.concatenate([imag, real], axis=0)
                    )
                return carry

            lax.fori_loop(0, 2, face_maps, 0)

        for k in range(1, n_row):
            y_wait(k)
        sbuf[0] = (gbuf[row] + ybuf[lax.rem(row + 1, n_row)]) + (
            ybuf[lax.rem(row + 2, n_row)] + ybuf[lax.rem(row + 3, n_row)]
        )

        def spread(out, into, send_sem, recv_sem):
            def start(k, carry):
                other = lax.rem(col + k, n_col)
                pltpu.make_async_remote_copy(
                    src_ref=out.at[:, pl.ds(pl.multiple_of(other * 8, 8), 8)],
                    dst_ref=into.at[:, pl.ds(pl.multiple_of(col * 8, 8), 8)],
                    send_sem=send_sem.at[other],
                    recv_sem=recv_sem.at[col],
                    device_id=(row, other),
                    device_id_type=MESH,
                ).start()
                return carry

            lax.fori_loop(1, n_col, start, 0)
            own = pl.ds(pl.multiple_of(col * 8, 8), 8)
            into[:, own, :] = out[:, own, :]

        def collect(out, into, send_sem, recv_sem):
            def finish(k, carry):
                other = lax.rem(col + k, n_col)
                block = pl.ds(pl.multiple_of(other * 8, 8), 8)
                copy = pltpu.make_async_remote_copy(
                    src_ref=out.at[:, block],
                    dst_ref=into.at[:, block],
                    send_sem=send_sem.at[other],
                    recv_sem=recv_sem.at[other],
                    device_id=(row, other),
                    device_id_type=MESH,
                )
                copy.wait_recv()
                copy.wait_send()
                return carry

            lax.fori_loop(1, n_col, finish, 0)

        spread(sbuf, slots, c_send, c_recv)
        for k in range(1, n_row):
            y_copy(k).wait_send()

        @pl.when(step == 0)
        def _():
            def own_map(face, carry):
                real, imag = rin[face, :, 0:256], rin[face, :, 256:512]
                town[:, 0:256] += dot3(outf[face], jnp.concatenate([real, -imag], axis=0))
                town[:, 256:512] += dot3(outf[face], jnp.concatenate([imag, real], axis=0))
                return carry

            town[...] = jnp.zeros_like(town)
            lax.fori_loop(0, 2, own_map, 0)

        collect(sbuf, slots, c_send, c_recv)

        def face_copy(face):
            other = up if face == 1 else down
            return pltpu.make_async_remote_copy(
                src_ref=faces.at[face],
                dst_ref=nbuf.at[1 - face],
                send_sem=f_send.at[face],
                recv_sem=f_recv.at[1 - face],
                device_id=(other // n_col, lax.rem(other, n_col)),
                device_id_type=MESH,
            )

        for face in range(2):
            faces[face] = dot3(rin[face], stacked(slots[0]))
            face_copy(face).start()
        cur[...] = dot3(town[...], stacked(slots[0]))
        for face in range(2):
            face_copy(1 - face).wait_recv()
            exists = (device > 0) if face == 0 else (device < total - 1)
            near = jnp.where(exists, nbuf[face], 0.0)
            cur[...] += dot3(orob[face], stacked(near))
        for face in range(2):
            face_copy(face).wait_send()

        def z_copy(k, receive):
            other = lax.rem(row + k, n_row)
            at = other if receive else row
            return pltpu.make_async_remote_copy(
                src_ref=curh.at[:, pl.ds(pl.multiple_of(other * 64, 64), 64)],
                dst_ref=zbuf.at[:, pl.ds(pl.multiple_of(at * 64, 64), 64)],
                send_sem=z_send.at[k],
                recv_sem=z_recv.at[at],
                device_id=(other, col),
                device_id_type=MESH,
            )

        for lane in range(2):
            curh[lane] = cur[:, lane * 128 : lane * 128 + 128]
        for k in (2, 1, 3):
            z_copy(k, False).start()
        own = pl.ds(pl.multiple_of(row * 64, 64), 64)
        zbuf[:, own, :] = curh[:, own, :]
        for k in range(1, n_row):
            z_copy(k, True).wait_recv()
        for source in range(n_row):
            for j in range(2):
                for lane in range(2):
                    zz[lane, pl.ds(source * 2 + j, n_col, stride=8), :] = zbuf[
                        lane, pl.ds(source * 64 + j, n_col, stride=2), :
                    ]
        spread(zz, fin, e_send, e_recv)
        for k in range(1, n_row):
            z_copy(k, False).wait_send()
        onehot = jnp.where(
            sid_ref[...] == lax.broadcasted_iota(jnp.int32, (128, 256), 0), 1.0, 0.0
        ).astype(jnp.bfloat16)
        collect(zz, fin, e_send, e_recv)
        back = pick(onehot, jnp.concatenate([fin[0], fin[1]], axis=1))
        basis[step + 1] = back

        @pl.when(step == 0)
        def _():
            vfull[col] = back * SCALE

    @pl.loop(0, ITERS)
    def _(step):
        operate(step)

    waves = out_ref.shape[1] // 2
    u0, b0, b1 = basis[0], basis[1], basis[2]
    sums = [square_terms(u0, waves), *inner_terms(u0, b0, waves), square_terms(b0, waves)]
    sums += [*inner_terms(u0, b1, waves), *inner_terms(b0, b1, waves), square_terms(b1, waves)]
    gram[...] = jnp.zeros_like(gram)
    for i, line in enumerate(sums):
        gram[pl.ds(i, 1), :] = line[None, :]

    def gy_copy(k, receive):
        other = lax.rem(row + k, n_row)
        at = other if receive else row
        return pltpu.make_async_remote_copy(
            src_ref=gram,
            dst_ref=gy.at[at],
            send_sem=gy_send.at[k],
            recv_sem=gy_recv.at[at],
            device_id=(other, col),
            device_id_type=MESH,
        )

    def gc_copy(k, receive):
        other = lax.rem(col + k, n_col)
        at = other if receive else col
        return pltpu.make_async_remote_copy(
            src_ref=gram2,
            dst_ref=gc.at[at],
            send_sem=gc_send.at[k],
            recv_sem=gc_recv.at[at],
            device_id=(row, other),
            device_id_type=MESH,
        )

    for k in (2, 1, 3):
        gy_copy(k, False).start()
    gy[row] = gram[...]
    for k in range(1, n_row):
        gy_copy(k, True).wait_recv()
    for k in range(1, n_row):
        gy_copy(k, False).wait_send()
    gram2[...] = (gy[0] + gy[1]) + (gy[2] + gy[3])

    @pl.loop(1, n_col)
    def _(k):
        gc_copy(k, False).start()

    gc[col] = gram2[...]

    @pl.loop(1, n_col)
    def _(k):
        gc_copy(k, True).wait_recv()

    gram[...] = jnp.sum(gc[...], axis=0)
    first, second = krylov_coefficients([gram[pl.ds(i, 1), :] for i in range(9)])
    out_ref[...] = scale_vector(basis[0], first, waves) + scale_vector(basis[1], second, waves)

    @pl.loop(1, n_col)
    def _(k):
        gc_copy(k, False).wait_send()


def on_device(
    rhs, dense, inflow, robin, outflow, trace_row, trace_count, current_row, current_count
):
    n_row = lax.axis_size("row")
    n_col = lax.axis_size("col")
    row_at = lax.axis_index("row")
    col_at = lax.axis_index("col")
    device_at = row_at * n_col + col_at
    tpair = trace_row.shape[2]
    tback = current_row.shape[2]

    def live(rows, counts, at):
        own = lax.dynamic_index_in_dim(rows, at, 0, keepdims=False)
        count = lax.dynamic_index_in_dim(counts, at, 0, keepdims=False)
        slot = jnp.arange(rows.shape[2], dtype=jnp.int32)[None, :]
        return jnp.where(slot < count[:, None], own, -1)

    tid = live(trace_row, trace_count, col_at).reshape(-1, 1)
    sid = live(current_row, current_count, device_at)
    sid = sid.reshape(n_row, n_col, tback).transpose(1, 0, 2).reshape(1, -1)
    f32 = jnp.float32
    vmem = pltpu.VMEM
    dma = pltpu.SemaphoreType.DMA
    any_spec = pl.BlockSpec(memory_space=pl.ANY)
    vmem_spec = pl.BlockSpec(memory_space=pltpu.VMEM)
    return pl.pallas_call(
        functools.partial(kernel, n_row, n_col),
        out_shape=jax.ShapeDtypeStruct(rhs.shape, f32),
        in_specs=[any_spec] * 5 + [vmem_spec] * 2,
        out_specs=vmem_spec,
        scratch_shapes=[
            vmem((32, 128, 256), f32),
            vmem((32, 512, 256), f32),
            vmem((512, 256), f32),
            vmem((1024, 512), jnp.bfloat16),
            vmem((4, 256, 256), f32),
            vmem((4, 256, 256), f32),
            vmem((1, 256, 256), f32),
            vmem((1, 256, 256), f32),
            vmem((2, 512, 512), f32),
            vmem((2, 512, 1024), f32),
            vmem((2, 256, 1024), f32),
            vmem((2, 512, 512), f32),
            vmem((2, 256, 1024), f32),
            vmem((256, 512), f32),
            vmem((2, 512, 256), f32),
            vmem((2, 512, 256), f32),
            vmem((256, 256), f32),
            vmem((2, 256, 128), f32),
            vmem((2, 256, 128), f32),
            vmem((2, 256, 128), f32),
            vmem((2, 256, 128), f32),
            vmem((3, 128, 256), f32),
            vmem((16, 128), f32),
            vmem((4, 16, 128), f32),
            vmem((16, 128), f32),
            vmem((32, 16, 128), f32),
            dma((14,)), dma((2, 32)), dma((36,)), dma((32, 2)), dma((4,)), dma((4,)),
            dma((32,)), dma((32,)), dma((2,)), dma((2,)), dma((4,)), dma((4,)),
            dma((32,)), dma((32,)), dma((4,)), dma((4,)), dma((32,)), dma((32,)),
        ],
        compiler_params=pltpu.CompilerParams(
            collective_id=0, has_side_effects=True, vmem_limit_bytes=62 * 1024 * 1024
        ),
        name="gmres",
    )(rhs, dense, inflow, robin, outflow, tid, sid)


def solution(mesh):
    placed = (
        P(("row", "col"), None),
        P(None, "col", "row"),
        P(("row", "col"), None, None, None, None),
        P(("row", "col"), None, None, None, None),
        P(("row", "col"), None, None, None),
        P(),
        P(),
        P(),
        P(),
    )
    return jax.shard_map(
        on_device, mesh=mesh, in_specs=placed, out_specs=P(("row", "col"), None), check_vma=False
    )
```

```python
import functools

import jax
import jax.numpy as jnp
from jax import lax
from jax.experimental import pallas as pl
from jax.experimental.pallas import tpu as pltpu
from jax.sharding import PartitionSpec as P

ITERS = 2


EPS = 1e-06
SCALE = 2.0**-24
MESH = pl.DeviceIdType.MESH


def scale_vector(vector, coef, waves):
    real_part = vector[:, :waves]
    imag_part = vector[:, waves:]
    return jnp.concatenate(
        [coef[0] * real_part - coef[1] * imag_part, coef[0] * imag_part + coef[1] * real_part],
        axis=1,
    )


def inner_terms(left, right, waves):
    left_real, left_imag = (left[:, :waves], left[:, waves:])
    right_real, right_imag = (right[:, :waves], right[:, waves:])
    return (
        jnp.sum(left_real * right_real + left_imag * right_imag, axis=0),
        jnp.sum(left_real * right_imag - left_imag * right_real, axis=0),
    )


def square_terms(vector, waves):
    halves = jnp.sum(vector * vector, axis=0)
    return halves[:waves] + halves[waves:]


def cmul(first, second):
    return (
        first[0] * second[0] - first[1] * second[1],
        first[0] * second[1] + first[1] * second[0],
    )


def cconj(first):
    return (first[0], -first[1])


def csub(first, second):
    return (first[0] - second[0], first[1] - second[1])


def cadd(first, second):
    return (first[0] + second[0], first[1] + second[1])


def cdiv(first, second):
    denom = second[0] * second[0] + second[1] * second[1]
    numer = cmul(first, cconj(second))
    return (numer[0] / denom, numer[1] / denom)


def solve_small(gram, target):
    size = len(target)
    gram = [list(line) for line in gram]
    target = list(target)
    for pivot in range(size):
        for lower in range(pivot + 1, size):
            factor = cdiv(gram[lower][pivot], gram[pivot][pivot])
            for other in range(pivot, size):
                gram[lower][other] = csub(gram[lower][other], cmul(factor, gram[pivot][other]))
            target[lower] = csub(target[lower], cmul(factor, target[pivot]))
    result = [None] * size
    for pivot in reversed(range(size)):
        summed = target[pivot]
        for other in range(pivot + 1, size):
            summed = csub(summed, cmul(gram[pivot][other], result[other]))
        result[pivot] = cdiv(summed, gram[pivot][pivot])
    return result


def least_squares(hess, beta, steps):
    zero_pair = (jnp.zeros_like(beta), jnp.zeros_like(beta))
    gram = []
    for first in range(steps):
        line = []
        for second in range(steps):
            summed = zero_pair
            for height in range(steps + 1):
                summed = cadd(
                    summed,
                    cmul(
                        cconj(hess.get((height, first), zero_pair)),
                        hess.get((height, second), zero_pair),
                    ),
                )
            line.append(summed)
        gram.append(line)
    target = [
        cmul(cconj(hess.get((0, first), zero_pair)), (beta, jnp.zeros_like(beta)))
        for first in range(steps)
    ]
    return solve_small(gram, target)


def turned(vector):
    waves = vector.shape[-1] // 2
    return jnp.concatenate([-vector[..., waves:], vector[..., :waves]], axis=-1)


def conj_mul(first, second):
    return cmul(cconj(first), second)


def krylov_coefficients(sums):
    norm0, p_real, p_imag, norm1, t_real, t_imag, s_real, s_imag, norm2 = sums
    zero = jnp.zeros_like(norm0)
    beta2 = norm0 + EPS
    beta = jnp.sqrt(beta2)
    unit = norm0 / beta2
    lack = EPS / beta2
    p = (p_real / beta2, p_imag / beta2)
    q = norm1 / beta2
    back = 1.0 / SCALE
    t = ((t_real / beta2) * back, (t_imag / beta2) * back)
    s = ((s_real / beta2) * back, (s_imag / beta2) * back)
    z = ((norm2 / beta2) * back) * back
    p_abs = p[0] * p[0] + p[1] * p[1]
    h00 = (unit + p[0], p[1])
    h10 = jnp.sqrt(unit * lack + 2.0 * lack * p[0] + (q - p_abs) + EPS)
    a = 1.0 / h10
    g = (lack - p[0], -p[1])
    g_abs = g[0] * g[0] + g[1] * g[1]
    gp = cmul(g, p)
    h01 = (
        a * (lack * h00[0] + (t[0] + gp[0])),
        a * (lack * h00[1] + (t[1] + gp[1])),
    )
    short = a * a * (lack * (1.0 - lack) * (unit + 2.0 * p[0]) + lack * p_abs + EPS)
    length = 1.0 - short
    gt = conj_mul(g, t)
    m = (
        a * a * (s[0] + g[0] * q + gt[0] + g_abs * p[0]),
        a * a * (s[1] + g[1] * q + gt[1] + g_abs * p[1]),
    )
    spread = a * a * (z + 2.0 * conj_mul(g, s)[0] + g_abs * q)
    h11 = (length + m[0], m[1])
    remain = length * short + 2.0 * short * m[0] + (spread - m[0] * m[0] - m[1] * m[1])
    remain = remain - h01[0] * h01[0] - h01[1] * h01[1]
    h21 = jnp.sqrt(remain + EPS)
    hess = {(0, 0): h00, (1, 0): (h10, zero), (0, 1): h01, (1, 1): h11, (2, 1): (h21, zero)}
    y0, y1 = least_squares(hess, beta, ITERS)
    ya = (y1[0] * a, y1[1] * a)
    yg = cmul(ya, g)
    return ((y0[0] + yg[0]) / beta, (y0[1] + yg[1]) / beta), (ya[0] / beta, ya[1] / beta)


def split(x):
    high = x.astype(jnp.bfloat16)
    return high, (x - high.astype(jnp.float32)).astype(jnp.bfloat16)


def mm(a, b):
    return jnp.dot(a, b, preferred_element_type=jnp.float32)


def dot3(a, b):
    a_high, a_low = split(a)
    b_high, b_low = split(b)
    return mm(a_high, b_high) + (mm(a_high, b_low) + mm(a_low, b_high))


def pick(onehot, x):
    high, low = split(x)
    return mm(onehot, high) + mm(onehot, low)


def stacked(x):
    return jnp.concatenate([x, turned(x)], axis=0)


EVENTS = [
    (-1, 0, 0), (1, 0, 1), (0, -1, 0), (0, 1, 1), (-1, 0, 1), (1, 0, 0), (0, -1, 1), (0, 1, 0),
    (2, 0, 0), (2, 0, 1), (-1, -1, 0), (1, 1, 1), (1, -1, 1), (-1, 1, 0), (0, 2, 0), (0, 2, 1),
    (-1, -1, 1), (1, 1, 0), (1, -1, 0), (-1, 1, 1), (-1, 2, 0), (1, 2, 1), (2, -1, 0), (2, 1, 1),
    (2, -1, 1), (2, 1, 0), (1, 2, 0), (-1, 2, 1), (2, 2, 0), (2, 2, 1),
]


def kernel(
    n_row, n_col,
    rhs_hbm, dense_hbm, inflow_hbm, robin_hbm, outflow_hbm,
    trow_hbm, tcount_hbm, crow_hbm, ccount_hbm,
    out_ref,
    vfull, dstage, acc, gmat, smat, gbuf, ybuf, rbuf, rsum, sbuf, slots, infl, rob, outf,
    rin, orob, orecv, town, tmap, faces, nbuf, cur, curh, zbuf, zz, fin, basis, gram, gy, gram2, gc,
    trow, tcount, crow, ccount,
    load_sem, dsem, ag_send, ag_recv, y_send, y_recv, c_send, c_recv,
    o_send, o_recv, f_send, f_recv, z_send, z_recv, e_send, e_recv, gy_send, gy_recv, gc_send, gc_recv,
):
    row = lax.axis_index("row")
    col = lax.axis_index("col")
    device = row * n_col + col
    total = n_row * n_col
    up = lax.rem(device + 1, total)
    down = lax.rem(device + total - 1, total)
    z = col // 8
    x = lax.rem(col // 2, 4)
    core = lax.rem(col, 2)
    stride_a = 8 - 6 * core
    stride_b = 2 + 6 * core
    at_a = z * (1 - core) + x * core
    at_b = x * (1 - core) + z * core

    def mine(da, db):
        return lax.rem(at_a + (da + 4), 4) * stride_a + lax.rem(at_b + (db + 4), 4) * stride_b + core

    def theirs(da, db):
        return (
            lax.rem(at_b + (da + 4), 4) * stride_b
            + lax.rem(at_a + (db + 4), 4) * stride_a
            + (1 - core)
        )

    partner = col + 1 - 2 * core
    half_rows = vfull.shape[1] // 2

    loads = [
        pltpu.make_async_copy(rhs_hbm, vfull.at[col], load_sem.at[0]),
        pltpu.make_async_copy(rhs_hbm, basis.at[0], load_sem.at[1]),
    ]
    tables = [
        pltpu.make_async_copy(trow_hbm.at[col], trow, load_sem.at[14]),
        pltpu.make_async_copy(tcount_hbm, tcount, load_sem.at[15]),
        pltpu.make_async_copy(crow_hbm.at[device], crow, load_sem.at[16]),
        pltpu.make_async_copy(ccount_hbm, ccount, load_sem.at[17]),
    ]
    for copy in loads + tables:
        copy.start()

    def dense_copy(part, index):
        return pltpu.make_async_copy(
            dense_hbm.at[part, :, pl.ds(pl.multiple_of(index * 128, 128), 128)],
            dstage.at[index, :, pl.ds(part * 128, 128)],
            dsem.at[part, index],
        )

    inner, outer = [], []
    for face in range(2):
        for part in range(2):
            inner.append(
                pltpu.make_async_copy(
                    inflow_hbm.at[0, face, part],
                    infl.at[face, :, pl.ds(part * 256, 256)],
                    load_sem.at[2 + len(inner)],
                )
            )
            outer.append(
                pltpu.make_async_copy(
                    robin_hbm.at[0, face, part],
                    rob.at[face, :, pl.ds(part * 512, 512)],
                    load_sem.at[6 + len(outer)],
                )
            )
            outer.append(
                pltpu.make_async_copy(
                    outflow_hbm.at[0, part, :, pl.ds(face * 512, 512)],
                    outf.at[face, :, pl.ds(part * 512, 512)],
                    load_sem.at[6 + len(outer)],
                )
            )
    dense_copy(0, col).start()
    dense_copy(1, col).start()
    for copy in outer:
        copy.start()

    @pl.loop(1, n_col)
    def _(k):
        index = lax.rem(col + k, n_col)
        dense_copy(0, index).start()
        dense_copy(1, index).start()

    for copy in inner:
        copy.start()

    barrier = pltpu.get_barrier_semaphore()

    @pl.loop(1, n_col)
    def _(k):
        other = lax.rem(col + k, n_col)
        pl.semaphore_signal(barrier, inc=1, device_id=(row, other), device_id_type=MESH)

    for k in range(1, n_row):
        other = lax.rem(row + k, n_row)
        pl.semaphore_signal(barrier, inc=1, device_id=(other, col), device_id_type=MESH)
    for other in (up, down):
        pl.semaphore_signal(
            barrier,
            inc=1,
            device_id=(other // n_col, lax.rem(other, n_col)),
            device_id_type=MESH,
        )

    for copy in tables:
        copy.wait()
    f32, i32, b16 = jnp.float32, jnp.int32, jnp.bfloat16
    slot = lax.broadcasted_iota(i32, (8, 128), 0)
    traced = jnp.where(slot < tcount[pl.ds(col, 1), :], trow[...], -1)
    traced = jnp.concatenate([traced, jnp.zeros((120, 128), i32)], axis=0)
    at_row = lax.broadcasted_iota(i32, (1024, 128), 0)
    at_lane = lax.broadcasted_iota(i32, (1024, 128), 1)
    expand = jnp.where(at_row // 8 == at_lane, 1.0, 0.0).astype(b16)
    across = (((1,), (1,)), ((), ()))

    def spread_rows(x):
        return lax.dot_general(
            expand, x.astype(f32).astype(b16), across, preferred_element_type=f32
        )

    table = 16.0 * spread_rows(traced >> 4) + spread_rows(traced & 15)
    row_id = jnp.sum(jnp.where(at_row % 8 == at_lane, table, 0.0), axis=1, keepdims=True)
    gmat[...] = jnp.where(
        row_id.astype(i32) == lax.broadcasted_iota(i32, gmat.shape, 1), 1.0, 0.0
    ).astype(b16)
    slot = lax.broadcasted_iota(i32, (2, 128), 0)
    given = jnp.where(slot < ccount[pl.ds(device, 1), :], crow[...], -1)
    given = jnp.concatenate([given, jnp.zeros((14, 128), i32)], axis=0)
    at_row = lax.broadcasted_iota(i32, (128, 256), 0)
    at_lane = lax.broadcasted_iota(i32, (128, 256), 1)
    order = jnp.where(at_row == (at_lane // 2 % 4) * 32 + at_lane // 8, 1.0, 0.0).astype(b16)
    table = mm(given.astype(f32).astype(b16), order)
    lane = lax.broadcasted_iota(i32, (1, 256), 1)
    target = jnp.where(lane % 2 == 0, table[0:1, :], table[1:2, :])
    smat[...] = jnp.where(
        target.astype(i32) == lax.broadcasted_iota(i32, smat.shape, 0), 1.0, 0.0
    ).astype(b16)

    pl.semaphore_wait(barrier, n_col - 1 + n_row - 1 + 2)
    for copy in loads:
        copy.wait()

    def sign(part):
        return (2 * part - 1).astype(jnp.float32)

    def outer_map(i, carry):
        face, tile, part = i // 4, i // 2 % 2, i % 2
        here = pl.multiple_of(part * 512 + tile * 256, 256)
        there = pl.multiple_of((1 - part) * 512 + tile * 256, 256)
        pair = [rob[face, :, pl.ds(here, 256)], rob[face, :, pl.ds(there, 256)] * sign(part)]
        orob[face, :, pl.ds(here, 256)] = dot3(outf[face], jnp.concatenate(pair, axis=0))
        return carry

    def halves(ref, face, part):
        here = ref[face, :, pl.ds(pl.multiple_of(part * 256, 256), 256)]
        there = ref[face, :, pl.ds(pl.multiple_of((1 - part) * 256, 256), 256)]
        return jnp.concatenate([here, there * sign(part)], axis=0)

    def inner_map(i, carry):
        face, part = i // 2, i % 2
        at = pl.ds(pl.multiple_of(part * 256, 256), 256)
        rin[face, :, at] = dot3(rob[face], halves(infl, face, part))
        return carry

    def own_map(part, carry):
        at = pl.ds(pl.multiple_of(part * 256, 256), 256)
        town[:, at] = dot3(outf[0], halves(rin, 0, part)) + dot3(outf[1], halves(rin, 1, part))
        return carry

    def side_map(i, carry):
        face, part = i // 2, i % 2
        at = pl.ds(pl.multiple_of(part * 256, 256), 256)
        tmap[face, :, at] = dot3(orecv[face], halves(rin, face, part))
        return carry

    def side_copy(source, target, send_sem, recv_sem, face):
        other = up if face == 1 else down
        return pltpu.make_async_remote_copy(
            src_ref=source.at[face],
            dst_ref=target.at[1 - face],
            send_sem=send_sem.at[face],
            recv_sem=recv_sem.at[1 - face],
            device_id=(other // n_col, lax.rem(other, n_col)),
            device_id_type=MESH,
        )

    def operate(step):
        sends = []

        def send(index, target, half):
            ref = vfull.at[index, pl.ds(half * half_rows, half_rows)]
            copy = pltpu.make_async_remote_copy(
                src_ref=ref,
                dst_ref=ref,
                send_sem=ag_send.at[len(sends)],
                recv_sem=ag_recv.at[index, half],
                device_id=(row, target),
                device_id_type=MESH,
            )
            copy.start()
            sends.append(copy)

        def await_half(index, half):
            ref = vfull.at[index, pl.ds(half * half_rows, half_rows)]
            pltpu.make_async_remote_copy(
                src_ref=ref, dst_ref=ref, send_sem=ag_send.at[0],
                recv_sem=ag_recv.at[index, half],
                device_id=(row, partner), device_id_type=MESH,
            ).wait_recv()

        def multiply(index):
            @pl.when(step == 0)
            def _():
                dense_copy(0, index).wait()
                dense_copy(1, index).wait()

            acc[...] += dot3(dstage[index], stacked(vfull[index]))

        acc[...] = jnp.zeros_like(acc)
        for half in range(2):
            send(col, mine(1, 0), half)
            send(col, mine(-1, 0), 1 - half)
        for half in range(2):
            send(col, mine(0, 1), half)
            send(col, mine(0, -1), 1 - half)
        for half in range(2):
            send(col, partner, half)
        multiply(col)

        @pl.when(step == 0)
        def _():
            for copy in outer:
                copy.wait()
            lax.fori_loop(0, 3, outer_map, 0)

        ready, seen, done = [(0, 0)], {}, 1
        for number, (da, db, half) in enumerate(EVENTS):
            index = mine(da, db)
            await_half(index, half)
            if db == 0:
                if da == -1 and half == 0:
                    send(index, mine(1, 0), half)
                elif da == 1 and half == 1:
                    send(index, mine(-1, 0), half)
                send(index, mine(0, 1), half)
                send(index, mine(0, -1), half)
            elif db == -1 and half == 0:
                send(index, mine(0, 1), half)
            elif db == 1 and half == 1:
                send(index, mine(0, -1), half)
            send(index, partner, half)
            seen[da, db] = seen.get((da, db), 0) + 1
            if seen[da, db] == 2:
                ready.append((da, db))
            if number == 3:

                @pl.when(step == 0)
                def _():
                    lax.fori_loop(3, 6, outer_map, 0)

            if number == 9:

                @pl.when(step == 0)
                def _():
                    lax.fori_loop(6, 8, outer_map, 0)

            last = number == len(EVENTS) - 1
            if number % 2 == 1:
                for _ in range(len(ready) - done if last else min(2, len(ready) - done)):
                    index, late = mine(*ready[done]), theirs(*ready[done - 1])
                    for half in range(2):
                        await_half(late, half)

                    def two(j, carry, index=index, late=late):
                        multiply(index * (1 - j) + late * j)
                        return carry

                    lax.fori_loop(0, 2, two, 0)
                    done += 1
        late = theirs(*ready[-1])
        for half in range(2):
            await_half(late, half)
        multiply(late)
        for copy in sends:
            copy.wait_send()

        above, below = lax.rem(row + 1, n_row), lax.rem(row + 3, n_row)
        low, high = pl.ds(0, 128), pl.ds(128, 128)

        def y_copy(number, source, target, other):
            return pltpu.make_async_remote_copy(
                src_ref=source,
                dst_ref=target,
                send_sem=y_send.at[number],
                recv_sem=y_recv.at[number],
                device_id=(other, col),
                device_id_type=MESH,
            )

        far = lax.rem(row + 2, n_row)
        y_copies = [
            y_copy(0, gbuf.at[far, low], rbuf.at[0], above),
            y_copy(1, gbuf.at[far, high], rbuf.at[1], below),
            y_copy(2, gbuf.at[above, high], ybuf.at[0, high], above),
            y_copy(3, gbuf.at[below, low], ybuf.at[1, low], below),
            y_copy(4, rsum.at[0], ybuf.at[0, low], above),
            y_copy(5, rsum.at[1], ybuf.at[1, high], below),
        ]

        @pl.when(step == 0)
        def _():
            for face in range(2):
                side_copy(orob, orecv, o_send, o_recv, face).start()

        def trace(other):
            rows = pl.ds(pl.multiple_of(other * 256, 256), 256)
            gbuf[other] = pick(gmat[rows, :], acc[...])

        trace(far)
        y_copies[0].start()
        y_copies[1].start()
        trace(above)
        y_copies[2].start()
        trace(below)
        y_copies[3].start()
        trace(row)
        y_copies[0].wait_recv()
        rsum[0] = gbuf[above, 0:128] + rbuf[0]
        y_copies[4].start()
        y_copies[1].wait_recv()
        rsum[1] = gbuf[below, 128:256] + rbuf[1]
        y_copies[5].start()

        @pl.when(step == 0)
        def _():
            for copy in inner:
                copy.wait()
            lax.fori_loop(0, 4, inner_map, 0)

        for copy in y_copies[2:]:
            copy.wait_recv()
        sbuf[0] = gbuf[row] + (ybuf[0] + ybuf[1])

        def spread(out, into, send_sem, recv_sem):
            def start(k, carry):
                other = lax.rem(col + k, n_col)
                pltpu.make_async_remote_copy(
                    src_ref=out.at[:, pl.ds(pl.multiple_of(other * 8, 8), 8)],
                    dst_ref=into.at[:, pl.ds(pl.multiple_of(col * 8, 8), 8)],
                    send_sem=send_sem.at[other],
                    recv_sem=recv_sem.at[col],
                    device_id=(row, other),
                    device_id_type=MESH,
                ).start()
                return carry

            lax.fori_loop(1, n_col, start, 0)
            own = pl.ds(pl.multiple_of(col * 8, 8), 8)
            into[:, own, :] = out[:, own, :]

        def collect(out, into, send_sem, recv_sem):
            def finish(k, carry):
                other = lax.rem(col + k, n_col)
                block = pl.ds(pl.multiple_of(other * 8, 8), 8)
                copy = pltpu.make_async_remote_copy(
                    src_ref=out.at[:, block],
                    dst_ref=into.at[:, block],
                    send_sem=send_sem.at[other],
                    recv_sem=recv_sem.at[other],
                    device_id=(row, other),
                    device_id_type=MESH,
                )
                copy.wait_recv()
                copy.wait_send()
                return carry

            lax.fori_loop(1, n_col, finish, 0)

        spread(sbuf, slots, c_send, c_recv)
        for copy in y_copies:
            copy.wait_send()

        @pl.when(step == 0)
        def _():
            lax.fori_loop(0, 2, own_map, 0)
            for face in range(2):
                side_copy(orob, orecv, o_send, o_recv, face).wait_send()
                side_copy(orob, orecv, o_send, o_recv, 1 - face).wait_recv()
            lax.fori_loop(0, 4, side_map, 0)

        collect(sbuf, slots, c_send, c_recv)

        ahead = stacked(slots[0])
        for face in range(2):
            faces[face] = dot3(tmap[face], ahead)
            side_copy(faces, nbuf, f_send, f_recv, face).start()
        cur[...] = dot3(town[...], ahead)
        for face in range(2):
            side_copy(faces, nbuf, f_send, f_recv, 1 - face).wait_recv()
            exists = (device > 0) if face == 0 else (device < total - 1)
            cur[...] += jnp.where(exists, nbuf[face], 0.0)
        for face in range(2):
            side_copy(faces, nbuf, f_send, f_recv, face).wait_send()

        def z_copy(k, receive):
            other = lax.rem(row + k, n_row)
            at = other if receive else row
            return pltpu.make_async_remote_copy(
                src_ref=curh.at[:, pl.ds(pl.multiple_of(other * 64, 64), 64)],
                dst_ref=zbuf.at[:, pl.ds(pl.multiple_of(at * 64, 64), 64)],
                send_sem=z_send.at[k],
                recv_sem=z_recv.at[at],
                device_id=(other, col),
                device_id_type=MESH,
            )

        for lane in range(2):
            curh[lane] = cur[:, lane * 128 : lane * 128 + 128]
        for k in (2, 1, 3):
            z_copy(k, False).start()
        own = pl.ds(pl.multiple_of(row * 64, 64), 64)
        zbuf[:, own, :] = curh[:, own, :]
        for k in range(1, n_row):
            z_copy(k, True).wait_recv()
        for source in range(n_row):
            for j in range(2):
                for lane in range(2):
                    zz[lane, pl.ds(source * 2 + j, n_col, stride=8), :] = zbuf[
                        lane, pl.ds(source * 64 + j, n_col, stride=2), :
                    ]
        spread(zz, fin, e_send, e_recv)
        for k in range(1, n_row):
            z_copy(k, False).wait_send()
        collect(zz, fin, e_send, e_recv)
        back = pick(smat[...], jnp.concatenate([fin[0], fin[1]], axis=1))
        basis[step + 1] = back

        @pl.when(step == 0)
        def _():
            vfull[col] = back * SCALE

    @pl.loop(0, ITERS)
    def _(step):
        operate(step)

    waves = out_ref.shape[1] // 2
    u0, b0, b1 = basis[0], basis[1], basis[2]
    sums = [square_terms(u0, waves), *inner_terms(u0, b0, waves), square_terms(b0, waves)]
    sums += [*inner_terms(u0, b1, waves), *inner_terms(b0, b1, waves), square_terms(b1, waves)]
    gram[...] = jnp.zeros_like(gram)
    for i, line in enumerate(sums):
        gram[pl.ds(i, 1), :] = line[None, :]

    def gy_copy(k, receive):
        other = lax.rem(row + k, n_row)
        at = other if receive else row
        return pltpu.make_async_remote_copy(
            src_ref=gram,
            dst_ref=gy.at[at],
            send_sem=gy_send.at[k],
            recv_sem=gy_recv.at[at],
            device_id=(other, col),
            device_id_type=MESH,
        )

    def gc_copy(k, receive):
        other = lax.rem(col + k, n_col)
        at = other if receive else col
        return pltpu.make_async_remote_copy(
            src_ref=gram2,
            dst_ref=gc.at[at],
            send_sem=gc_send.at[k],
            recv_sem=gc_recv.at[at],
            device_id=(row, other),
            device_id_type=MESH,
        )

    for k in (2, 1, 3):
        gy_copy(k, False).start()
    gy[row] = gram[...]
    for k in range(1, n_row):
        gy_copy(k, True).wait_recv()
    for k in range(1, n_row):
        gy_copy(k, False).wait_send()
    gram2[...] = (gy[0] + gy[1]) + (gy[2] + gy[3])

    @pl.loop(1, n_col)
    def _(k):
        gc_copy(k, False).start()

    gc[col] = gram2[...]

    @pl.loop(1, n_col)
    def _(k):
        gc_copy(k, True).wait_recv()

    gram[...] = jnp.sum(gc[...], axis=0)
    first, second = krylov_coefficients([gram[pl.ds(i, 1), :] for i in range(9)])
    out_ref[...] = scale_vector(basis[0], first, waves) + scale_vector(basis[1], second, waves)

    @pl.loop(1, n_col)
    def _(k):
        gc_copy(k, False).wait_send()


def on_device(
    rhs, dense, inflow, robin, outflow, trace_row, trace_count, current_row, current_count
):
    n_row = lax.axis_size("row")
    n_col = lax.axis_size("col")
    f32 = jnp.float32
    vmem = pltpu.VMEM
    dma = pltpu.SemaphoreType.DMA
    any_spec = pl.BlockSpec(memory_space=pl.ANY)
    vmem_spec = pl.BlockSpec(memory_space=pltpu.VMEM)
    return pl.pallas_call(
        functools.partial(kernel, n_row, n_col),
        out_shape=jax.ShapeDtypeStruct(rhs.shape, f32),
        in_specs=[any_spec] * 9,
        out_specs=vmem_spec,
        scratch_shapes=[
            vmem((32, 128, 256), f32),
            vmem((32, 512, 256), f32),
            vmem((512, 256), f32),
            vmem((1024, 512), jnp.bfloat16),
            vmem((128, 256), jnp.bfloat16),
            vmem((4, 256, 256), f32),
            vmem((2, 256, 256), f32),
            vmem((2, 128, 256), f32),
            vmem((2, 128, 256), f32),
            vmem((1, 256, 256), f32),
            vmem((1, 256, 256), f32),
            vmem((2, 512, 512), f32),
            vmem((2, 512, 1024), f32),
            vmem((2, 256, 1024), f32),
            vmem((2, 512, 512), f32),
            vmem((2, 256, 1024), f32),
            vmem((2, 256, 1024), f32),
            vmem((256, 512), f32),
            vmem((2, 256, 512), f32),
            vmem((2, 256, 256), f32),
            vmem((2, 256, 256), f32),
            vmem((256, 256), f32),
            vmem((2, 256, 128), f32),
            vmem((2, 256, 128), f32),
            vmem((2, 256, 128), f32),
            vmem((2, 256, 128), f32),
            vmem((3, 128, 256), f32),
            vmem((16, 128), f32),
            vmem((4, 16, 128), f32),
            vmem((16, 128), f32),
            vmem((32, 16, 128), f32),
            vmem((8, 128), jnp.int32), vmem((32, 128), jnp.int32),
            vmem((2, 128), jnp.int32), vmem((128, 128), jnp.int32),
            dma((18,)), dma((2, 32)), dma((62,)), dma((32, 2)), dma((6,)), dma((6,)),
            dma((32,)), dma((32,)), dma((2,)), dma((2,)), dma((2,)), dma((2,)), dma((4,)), dma((4,)),
            dma((32,)), dma((32,)), dma((4,)), dma((4,)), dma((32,)), dma((32,)),
        ],
        compiler_params=pltpu.CompilerParams(
            collective_id=0, has_side_effects=True, vmem_limit_bytes=62 * 1024 * 1024
        ),
        name="gmres",
    )(
        rhs, dense, inflow, robin, outflow,
        trace_row.transpose(0, 2, 1), trace_count, current_row.transpose(0, 2, 1), current_count,
    )


def solution(mesh):
    placed = (
        P(("row", "col"), None),
        P(None, "col", "row"),
        P(("row", "col"), None, None, None, None),
        P(("row", "col"), None, None, None, None),
        P(("row", "col"), None, None, None),
        P(),
        P(),
        P(),
        P(),
    )
    return jax.shard_map(
        on_device, mesh=mesh, in_specs=placed, out_specs=P(("row", "col"), None), check_vma=False
    )
```

```python
import functools

import jax
import jax.numpy as jnp
from jax import lax
from jax.experimental import pallas as pl
from jax.experimental.pallas import tpu as pltpu
from jax.sharding import PartitionSpec as P

ITERS = 2


EPS = 1e-06
SCALE = 2.0**-24
MESH = pl.DeviceIdType.MESH


def scale_vector(vector, coef, waves):
    real_part = vector[:, :waves]
    imag_part = vector[:, waves:]
    return jnp.concatenate(
        [coef[0] * real_part - coef[1] * imag_part, coef[0] * imag_part + coef[1] * real_part],
        axis=1,
    )


def inner_terms(left, right, waves):
    left_real, left_imag = (left[:, :waves], left[:, waves:])
    right_real, right_imag = (right[:, :waves], right[:, waves:])
    return (
        jnp.sum(left_real * right_real + left_imag * right_imag, axis=0),
        jnp.sum(left_real * right_imag - left_imag * right_real, axis=0),
    )


def square_terms(vector, waves):
    halves = jnp.sum(vector * vector, axis=0)
    return halves[:waves] + halves[waves:]


def cmul(first, second):
    return (
        first[0] * second[0] - first[1] * second[1],
        first[0] * second[1] + first[1] * second[0],
    )


def cconj(first):
    return (first[0], -first[1])


def csub(first, second):
    return (first[0] - second[0], first[1] - second[1])


def cadd(first, second):
    return (first[0] + second[0], first[1] + second[1])


def cdiv(first, second):
    denom = second[0] * second[0] + second[1] * second[1]
    numer = cmul(first, cconj(second))
    return (numer[0] / denom, numer[1] / denom)


def solve_small(gram, target):
    size = len(target)
    gram = [list(line) for line in gram]
    target = list(target)
    for pivot in range(size):
        for lower in range(pivot + 1, size):
            factor = cdiv(gram[lower][pivot], gram[pivot][pivot])
            for other in range(pivot, size):
                gram[lower][other] = csub(gram[lower][other], cmul(factor, gram[pivot][other]))
            target[lower] = csub(target[lower], cmul(factor, target[pivot]))
    result = [None] * size
    for pivot in reversed(range(size)):
        summed = target[pivot]
        for other in range(pivot + 1, size):
            summed = csub(summed, cmul(gram[pivot][other], result[other]))
        result[pivot] = cdiv(summed, gram[pivot][pivot])
    return result


def least_squares(hess, beta, steps):
    zero_pair = (jnp.zeros_like(beta), jnp.zeros_like(beta))
    gram = []
    for first in range(steps):
        line = []
        for second in range(steps):
            summed = zero_pair
            for height in range(steps + 1):
                summed = cadd(
                    summed,
                    cmul(
                        cconj(hess.get((height, first), zero_pair)),
                        hess.get((height, second), zero_pair),
                    ),
                )
            line.append(summed)
        gram.append(line)
    target = [
        cmul(cconj(hess.get((0, first), zero_pair)), (beta, jnp.zeros_like(beta)))
        for first in range(steps)
    ]
    return solve_small(gram, target)


def turned(vector):
    waves = vector.shape[-1] // 2
    return jnp.concatenate([-vector[..., waves:], vector[..., :waves]], axis=-1)


def conj_mul(first, second):
    return cmul(cconj(first), second)


def krylov_coefficients(sums):
    norm0, p_real, p_imag, norm1, t_real, t_imag, s_real, s_imag, norm2 = sums
    zero = jnp.zeros_like(norm0)
    beta2 = norm0 + EPS
    beta = jnp.sqrt(beta2)
    unit = norm0 / beta2
    lack = EPS / beta2
    p = (p_real / beta2, p_imag / beta2)
    q = norm1 / beta2
    back = 1.0 / SCALE
    t = ((t_real / beta2) * back, (t_imag / beta2) * back)
    s = ((s_real / beta2) * back, (s_imag / beta2) * back)
    z = ((norm2 / beta2) * back) * back
    p_abs = p[0] * p[0] + p[1] * p[1]
    h00 = (unit + p[0], p[1])
    h10 = jnp.sqrt(unit * lack + 2.0 * lack * p[0] + (q - p_abs) + EPS)
    a = 1.0 / h10
    g = (lack - p[0], -p[1])
    g_abs = g[0] * g[0] + g[1] * g[1]
    gp = cmul(g, p)
    h01 = (
        a * (lack * h00[0] + (t[0] + gp[0])),
        a * (lack * h00[1] + (t[1] + gp[1])),
    )
    short = a * a * (lack * (1.0 - lack) * (unit + 2.0 * p[0]) + lack * p_abs + EPS)
    length = 1.0 - short
    gt = conj_mul(g, t)
    m = (
        a * a * (s[0] + g[0] * q + gt[0] + g_abs * p[0]),
        a * a * (s[1] + g[1] * q + gt[1] + g_abs * p[1]),
    )
    spread = a * a * (z + 2.0 * conj_mul(g, s)[0] + g_abs * q)
    h11 = (length + m[0], m[1])
    remain = length * short + 2.0 * short * m[0] + (spread - m[0] * m[0] - m[1] * m[1])
    remain = remain - h01[0] * h01[0] - h01[1] * h01[1]
    h21 = jnp.sqrt(remain + EPS)
    hess = {(0, 0): h00, (1, 0): (h10, zero), (0, 1): h01, (1, 1): h11, (2, 1): (h21, zero)}
    y0, y1 = least_squares(hess, beta, ITERS)
    ya = (y1[0] * a, y1[1] * a)
    yg = cmul(ya, g)
    return ((y0[0] + yg[0]) / beta, (y0[1] + yg[1]) / beta), (ya[0] / beta, ya[1] / beta)


def split(x):
    high = x.astype(jnp.bfloat16)
    return high, (x - high.astype(jnp.float32)).astype(jnp.bfloat16)


def mm(a, b):
    return jnp.dot(a, b, preferred_element_type=jnp.float32)


def dot3(a, b):
    a_high, a_low = split(a)
    b_high, b_low = split(b)
    return mm(a_high, b_high) + (mm(a_high, b_low) + mm(a_low, b_high))


def pick(onehot, x):
    high, low = split(x)
    return mm(onehot, high) + mm(onehot, low)


def stacked(x):
    return jnp.concatenate([x, turned(x)], axis=0)


LAG = 2
EVENTS = [
    (-1, 0, 0), (1, 0, 1), (0, -1, 0), (0, 1, 1), (-1, 0, 1), (1, 0, 0), (0, -1, 1), (0, 1, 0),
    (2, 0, 0), (2, 0, 1), (-1, -1, 0), (1, 1, 1), (1, -1, 1), (-1, 1, 0), (0, 2, 0), (0, 2, 1),
    (-1, -1, 1), (1, 1, 0), (1, -1, 0), (-1, 1, 1), (-1, 2, 0), (1, 2, 1), (2, -1, 0), (2, 1, 1),
    (2, -1, 1), (2, 1, 0), (1, 2, 0), (-1, 2, 1), (2, 2, 0), (2, 2, 1),
]


READY = [(0, 0)]
for _i, _event in enumerate(EVENTS):
    if _event[:2] in [_e[:2] for _e in EVENTS[:_i]]:
        READY.append(_event[:2])

OFFSETS = sorted(
    [(dz, dx, dk) for dz in range(4) for dx in range(4) for dk in range(2)],
    key=lambda o: -(min(o[0], 4 - o[0]) + min(o[1], 4 - o[1]) + 0.1 * o[2]),
)[:-1]


def kernel(
    n_row, n_col,
    rhs_hbm, dense_hbm, inflow_hbm, robin_hbm, outflow_hbm,
    trow_hbm, tcount_hbm, crow_hbm, ccount_hbm,
    out_ref,
    vfull, dstage, acc, gmat, smat, gbuf, ybuf, rbuf, rsum, sbuf, slots, infl, rob, outf,
    rin, orob, orecv, town, tmap, faces, nbuf, cur, curh, zbuf, zz, fin, basis, gram, gy, gram2, gc,
    trow, tcount, crow, ccount,
    load_sem, dsem, ag_send, ag_recv, y_send, y_recv, c_send, c_recv,
    o_send, o_recv, f_send, f_recv, z_send, z_recv, e_send, e_recv, gy_send, gy_recv, gc_send, gc_recv,
):
    row = lax.axis_index("row")
    col = lax.axis_index("col")
    device = row * n_col + col
    total = n_row * n_col
    up = lax.rem(device + 1, total)
    down = lax.rem(device + total - 1, total)
    z = col // 8
    x = lax.rem(col // 2, 4)
    core = lax.rem(col, 2)
    stride_a = 8 - 6 * core
    stride_b = 2 + 6 * core
    at_a = z * (1 - core) + x * core
    at_b = x * (1 - core) + z * core

    def mine(da, db):
        return lax.rem(at_a + (da + 4), 4) * stride_a + lax.rem(at_b + (db + 4), 4) * stride_b + core

    def theirs(da, db):
        return (
            lax.rem(at_b + (da + 4), 4) * stride_b
            + lax.rem(at_a + (db + 4), 4) * stride_a
            + (1 - core)
        )

    partner = col + 1 - 2 * core

    def offset_col(dz, dx, dk):
        return lax.rem(z + dz, 4) * 8 + lax.rem(x + dx, 4) * 2 + lax.rem(core + dk, 2)

    half_rows = vfull.shape[1] // 2

    loads = [
        pltpu.make_async_copy(rhs_hbm, vfull.at[col], load_sem.at[0]),
        pltpu.make_async_copy(rhs_hbm, basis.at[0], load_sem.at[1]),
    ]
    tables = [
        pltpu.make_async_copy(trow_hbm.at[col], trow, load_sem.at[14]),
        pltpu.make_async_copy(tcount_hbm, tcount, load_sem.at[15]),
        pltpu.make_async_copy(crow_hbm.at[device], crow, load_sem.at[16]),
        pltpu.make_async_copy(ccount_hbm, ccount, load_sem.at[17]),
    ]
    for copy in loads + tables:
        copy.start()

    def dense_copy(part, index):
        return pltpu.make_async_copy(
            dense_hbm.at[part, :, pl.ds(pl.multiple_of(index * 128, 128), 128)],
            dstage.at[index, :, pl.ds(part * 128, 128)],
            dsem.at[part, index],
        )

    inner, outer = [], []
    for face in range(2):
        for part in range(2):
            inner.append(
                pltpu.make_async_copy(
                    inflow_hbm.at[0, face, part],
                    infl.at[face, :, pl.ds(part * 256, 256)],
                    load_sem.at[2 + len(inner)],
                )
            )
            outer.append(
                pltpu.make_async_copy(
                    robin_hbm.at[0, face, part],
                    rob.at[face, :, pl.ds(part * 512, 512)],
                    load_sem.at[6 + len(outer)],
                )
            )
            outer.append(
                pltpu.make_async_copy(
                    outflow_hbm.at[0, part, :, pl.ds(face * 512, 512)],
                    outf.at[face, :, pl.ds(part * 512, 512)],
                    load_sem.at[6 + len(outer)],
                )
            )
    dense_copy(0, col).start()
    dense_copy(1, col).start()
    for copy in outer:
        copy.start()

    for number, spot in enumerate(READY):
        for index in ([] if number == 0 else [mine(*spot)]) + [theirs(*spot)]:
            dense_copy(0, index).start()
            dense_copy(1, index).start()
        if number == 6:
            for copy in inner:
                copy.start()


    barrier = pltpu.get_barrier_semaphore()

    @pl.loop(1, n_col)
    def _(k):
        other = lax.rem(col + k, n_col)
        pl.semaphore_signal(barrier, inc=1, device_id=(row, other), device_id_type=MESH)

    for k in range(1, n_row):
        other = lax.rem(row + k, n_row)
        pl.semaphore_signal(barrier, inc=1, device_id=(other, col), device_id_type=MESH)
    for other in (up, down):
        pl.semaphore_signal(
            barrier,
            inc=1,
            device_id=(other // n_col, lax.rem(other, n_col)),
            device_id_type=MESH,
        )

    for copy in tables:
        copy.wait()
    f32, i32, b16 = jnp.float32, jnp.int32, jnp.bfloat16
    slot = lax.broadcasted_iota(i32, (8, 128), 0)
    traced = jnp.where(slot < tcount[pl.ds(col, 1), :], trow[...], -1)
    traced = jnp.concatenate([traced, jnp.zeros((120, 128), i32)], axis=0)
    at_row = lax.broadcasted_iota(i32, (1024, 128), 0)
    at_lane = lax.broadcasted_iota(i32, (1024, 128), 1)
    expand = jnp.where(at_row // 8 == at_lane, 1.0, 0.0).astype(b16)
    across = (((1,), (1,)), ((), ()))

    def spread_rows(x):
        return lax.dot_general(
            expand, x.astype(f32).astype(b16), across, preferred_element_type=f32
        )

    table = 16.0 * spread_rows(traced >> 4) + spread_rows(traced & 15)
    row_id = jnp.sum(jnp.where(at_row % 8 == at_lane, table, 0.0), axis=1, keepdims=True)
    gmat[...] = jnp.where(
        row_id.astype(i32) == lax.broadcasted_iota(i32, gmat.shape, 1), 1.0, 0.0
    ).astype(b16)
    slot = lax.broadcasted_iota(i32, (2, 128), 0)
    given = jnp.where(slot < ccount[pl.ds(device, 1), :], crow[...], -1)
    given = jnp.concatenate([given, jnp.zeros((14, 128), i32)], axis=0)
    at_row = lax.broadcasted_iota(i32, (128, 256), 0)
    at_lane = lax.broadcasted_iota(i32, (128, 256), 1)
    order = jnp.where(at_row == (at_lane // 2 % 4) * 32 + at_lane // 8, 1.0, 0.0).astype(b16)
    table = mm(given.astype(f32).astype(b16), order)
    lane = lax.broadcasted_iota(i32, (1, 256), 1)
    target = jnp.where(lane % 2 == 0, table[0:1, :], table[1:2, :])
    smat[...] = jnp.where(
        target.astype(i32) == lax.broadcasted_iota(i32, smat.shape, 0), 1.0, 0.0
    ).astype(b16)

    pl.semaphore_wait(barrier, n_col - 1 + n_row - 1 + 2)
    for copy in loads:
        copy.wait()

    def sign(part):
        return (2 * part - 1).astype(jnp.float32)

    def outer_map(i, carry):
        face, tile, part = i // 4, i // 2 % 2, i % 2
        here = pl.multiple_of(part * 512 + tile * 256, 256)
        there = pl.multiple_of((1 - part) * 512 + tile * 256, 256)
        pair = [rob[face, :, pl.ds(here, 256)], rob[face, :, pl.ds(there, 256)] * sign(part)]
        orob[face, :, pl.ds(here, 256)] = dot3(outf[face], jnp.concatenate(pair, axis=0))
        return carry

    def halves(ref, face, part):
        here = ref[face, :, pl.ds(pl.multiple_of(part * 256, 256), 256)]
        there = ref[face, :, pl.ds(pl.multiple_of((1 - part) * 256, 256), 256)]
        return jnp.concatenate([here, there * sign(part)], axis=0)

    def inner_map(i, carry):
        face, part, rows = i // 4, i // 2 % 2, pl.ds(pl.multiple_of(i % 2 * 256, 256), 256)
        at = pl.ds(pl.multiple_of(part * 256, 256), 256)
        rin[face, rows, at] = dot3(rob[face, rows, :], halves(infl, face, part))
        return carry

    def own_map(part, carry):
        at = pl.ds(pl.multiple_of(part * 256, 256), 256)
        town[:, at] = dot3(outf[0], halves(rin, 0, part)) + dot3(outf[1], halves(rin, 1, part))
        return carry

    def side_map(i, carry):
        face, part = i // 2, i % 2
        at = pl.ds(pl.multiple_of(part * 256, 256), 256)
        tmap[face, :, at] = dot3(orecv[face], halves(rin, face, part))
        return carry

    def side_copy(source, target, send_sem, recv_sem, face):
        other = up if face == 1 else down
        return pltpu.make_async_remote_copy(
            src_ref=source.at[face],
            dst_ref=target.at[1 - face],
            send_sem=send_sem.at[face],
            recv_sem=recv_sem.at[1 - face],
            device_id=(other // n_col, lax.rem(other, n_col)),
            device_id_type=MESH,
        )

    waves = out_ref.shape[1] // 2

    def gy_copy(part, k, receive):
        other = lax.rem(row + k, n_row)
        at = other if receive else row
        return pltpu.make_async_remote_copy(
            src_ref=gram.at[part],
            dst_ref=gy.at[part, at],
            send_sem=gy_send.at[part, k],
            recv_sem=gy_recv.at[part, at],
            device_id=(other, col),
            device_id_type=MESH,
        )

    def gc_copy(part, offset, receive):
        other = offset_col(*offset)
        at = other if receive else col
        return pltpu.make_async_remote_copy(
            src_ref=gram2.at[part],
            dst_ref=gc.at[part, at],
            send_sem=gc_send.at[part, other],
            recv_sem=gc_recv.at[part, at],
            device_id=(row, other),
            device_id_type=MESH,
        )

    def over_row(part, lines):
        gram[part] = jnp.zeros((8, waves), jnp.float32)
        for i, line in enumerate(lines):
            gram[part, pl.ds(i, 1), :] = line[None, :]
        for k in (2, 1, 3):
            gy_copy(part, k, False).start()
        gy[part, row] = gram[part]

    def over_col(part):
        for k in range(1, n_row):
            gy_copy(part, k, True).wait_recv()
        for k in range(1, n_row):
            gy_copy(part, k, False).wait_send()
        gram2[part] = (gy[part, 0] + gy[part, 1]) + (gy[part, 2] + gy[part, 3])
        for offset in OFFSETS:
            gc_copy(part, offset, False).start()
        gc[part, col] = gram2[part]

    def finish_col(part):
        for offset in OFFSETS:
            gc_copy(part, offset, True).wait_recv()

    def operate(step):
        sends = []

        def send(index, target, half):
            ref = vfull.at[index, pl.ds(half * half_rows, half_rows)]
            copy = pltpu.make_async_remote_copy(
                src_ref=ref,
                dst_ref=ref,
                send_sem=ag_send.at[len(sends)],
                recv_sem=ag_recv.at[index, half],
                device_id=(row, target),
                device_id_type=MESH,
            )
            copy.start()
            sends.append(copy)

        def await_half(index, half):
            ref = vfull.at[index, pl.ds(half * half_rows, half_rows)]
            pltpu.make_async_remote_copy(
                src_ref=ref, dst_ref=ref, send_sem=ag_send.at[0],
                recv_sem=ag_recv.at[index, half],
                device_id=(row, partner), device_id_type=MESH,
            ).wait_recv()

        def multiply(index):
            @pl.when(step == 0)
            def _():
                dense_copy(0, index).wait()
                dense_copy(1, index).wait()

            acc[...] += dot3(dstage[index], stacked(vfull[index]))

        acc[...] = jnp.zeros_like(acc)
        for half in range(2):
            send(col, mine(1, 0), half)
            send(col, mine(-1, 0), 1 - half)
        for half in range(2):
            send(col, mine(0, 1), half)
            send(col, mine(0, -1), 1 - half)
        for half in range(2):
            send(col, partner, half)
        @pl.when(step == 1)
        def _():
            u0, b0 = basis[0], basis[1]
            lines = [square_terms(u0, waves), *inner_terms(u0, b0, waves), square_terms(b0, waves)]
            over_row(0, lines)

        multiply(col)

        @pl.when(step == 0)
        def _():
            for copy in outer:
                copy.wait()
            lax.fori_loop(0, 3, outer_map, 0)

        ready, seen, done = [(0, 0)], {}, 1
        for number, (da, db, half) in enumerate(EVENTS):
            index = mine(da, db)
            await_half(index, half)
            if db == 0:
                if da == -1 and half == 0:
                    send(index, mine(1, 0), half)
                elif da == 1 and half == 1:
                    send(index, mine(-1, 0), half)
                send(index, mine(0, 1), half)
                send(index, mine(0, -1), half)
            elif db == -1 and half == 0:
                send(index, mine(0, 1), half)
            elif db == 1 and half == 1:
                send(index, mine(0, -1), half)
            send(index, partner, half)
            seen[da, db] = seen.get((da, db), 0) + 1
            if seen[da, db] == 2:
                ready.append((da, db))
            work = {2: (outer_map, 3, 5), 3: (outer_map, 5, 6), 7: (outer_map, 6, 8)}
            work.update({9 + 2 * i: (inner_map, i, i + 1) for i in range(8)})
            if number in work:

                @pl.when(step == 0)
                def _(number=number):
                    if number == 9:
                        for copy in inner:
                            copy.wait()
                    fn, start, stop = work[number]
                    lax.fori_loop(start, stop, fn, 0)

            last = number == len(EVENTS) - 1
            if number % 2 == 1:
                for _ in range(len(ready) - done if last else min(2, len(ready) - done)):
                    index = mine(*ready[done])
                    if done < LAG:
                        multiply(index)
                        done += 1
                        continue
                    late = theirs(*ready[done - LAG])
                    for half in range(2):
                        await_half(late, half)

                    def two(j, carry, index=index, late=late):
                        multiply(index * (1 - j) + late * j)
                        return carry

                    lax.fori_loop(0, 2, two, 0)
                    done += 1
        for spot in ready[-LAG:]:
            late = theirs(*spot)
            for half in range(2):
                await_half(late, half)
            multiply(late)

        above, below = lax.rem(row + 1, n_row), lax.rem(row + 3, n_row)
        low, high = pl.ds(0, 128), pl.ds(128, 128)

        def y_copy(number, source, target, other):
            return pltpu.make_async_remote_copy(
                src_ref=source,
                dst_ref=target,
                send_sem=y_send.at[number],
                recv_sem=y_recv.at[number],
                device_id=(other, col),
                device_id_type=MESH,
            )

        far = lax.rem(row + 2, n_row)
        y_copies = [
            y_copy(0, gbuf.at[far, low], rbuf.at[0], above),
            y_copy(1, gbuf.at[far, high], rbuf.at[1], below),
            y_copy(2, gbuf.at[above, high], ybuf.at[0, high], above),
            y_copy(3, gbuf.at[below, low], ybuf.at[1, low], below),
            y_copy(4, rsum.at[0], ybuf.at[0, low], above),
            y_copy(5, rsum.at[1], ybuf.at[1, high], below),
        ]

        @pl.when(step == 0)
        def _():
            for face in range(2):
                side_copy(orob, orecv, o_send, o_recv, face).start()

        def trace(other):
            rows = pl.ds(pl.multiple_of(other * 256, 256), 256)
            gbuf[other] = pick(gmat[rows, :], acc[...])

        trace(far)
        y_copies[0].start()
        y_copies[1].start()
        trace(above)
        y_copies[2].start()
        trace(below)
        y_copies[3].start()
        trace(row)
        y_copies[0].wait_recv()
        rsum[0] = gbuf[above, 0:128] + rbuf[0]
        y_copies[4].start()
        y_copies[1].wait_recv()
        rsum[1] = gbuf[below, 128:256] + rbuf[1]
        y_copies[5].start()

        @pl.when(step == 0)
        def _():
            lax.fori_loop(0, 2, own_map, 0)

        @pl.when(step == 1)
        def _():
            over_col(0)

        for copy in y_copies[2:]:
            copy.wait_recv()
        sbuf[0] = gbuf[row] + (ybuf[0] + ybuf[1])

        def spread(out, into, send_sem, recv_sem):
            for offset in OFFSETS:
                other = offset_col(*offset)
                pltpu.make_async_remote_copy(
                    src_ref=out.at[:, pl.ds(pl.multiple_of(other * 8, 8), 8)],
                    dst_ref=into.at[:, pl.ds(pl.multiple_of(col * 8, 8), 8)],
                    send_sem=send_sem.at[other],
                    recv_sem=recv_sem.at[col],
                    device_id=(row, other),
                    device_id_type=MESH,
                ).start()
            own = pl.ds(pl.multiple_of(col * 8, 8), 8)
            into[:, own, :] = out[:, own, :]

        def collect(out, into, send_sem, recv_sem):
            def finish(k, carry):
                other = lax.rem(col + k, n_col)
                block = pl.ds(pl.multiple_of(other * 8, 8), 8)
                copy = pltpu.make_async_remote_copy(
                    src_ref=out.at[:, block],
                    dst_ref=into.at[:, block],
                    send_sem=send_sem.at[other],
                    recv_sem=recv_sem.at[other],
                    device_id=(row, other),
                    device_id_type=MESH,
                )
                copy.wait_recv()
                copy.wait_send()
                return carry

            lax.fori_loop(1, n_col, finish, 0)

        spread(sbuf, slots, c_send, c_recv)
        for copy in sends + y_copies:
            copy.wait_send()

        @pl.when(step == 0)
        def _():
            for face in range(2):
                side_copy(orob, orecv, o_send, o_recv, face).wait_send()
                side_copy(orob, orecv, o_send, o_recv, 1 - face).wait_recv()
            lax.fori_loop(0, 4, side_map, 0)

        collect(sbuf, slots, c_send, c_recv)

        ahead = stacked(slots[0])
        for face in range(2):
            faces[face] = dot3(tmap[face], ahead)
            side_copy(faces, nbuf, f_send, f_recv, face).start()
        cur[...] = dot3(town[...], ahead)
        for face in range(2):
            side_copy(faces, nbuf, f_send, f_recv, 1 - face).wait_recv()
            exists = (device > 0) if face == 0 else (device < total - 1)
            cur[...] += jnp.where(exists, nbuf[face], 0.0)
        for face in range(2):
            side_copy(faces, nbuf, f_send, f_recv, face).wait_send()

        def z_copy(k, receive):
            other = lax.rem(row + k, n_row)
            at = other if receive else row
            return pltpu.make_async_remote_copy(
                src_ref=curh.at[:, pl.ds(pl.multiple_of(other * 64, 64), 64)],
                dst_ref=zbuf.at[:, pl.ds(pl.multiple_of(at * 64, 64), 64)],
                send_sem=z_send.at[k],
                recv_sem=z_recv.at[at],
                device_id=(other, col),
                device_id_type=MESH,
            )

        for lane in range(2):
            curh[lane] = cur[:, lane * 128 : lane * 128 + 128]
        for k in (2, 1, 3):
            z_copy(k, False).start()
        own = pl.ds(pl.multiple_of(row * 64, 64), 64)
        zbuf[:, own, :] = curh[:, own, :]
        for k in range(1, n_row):
            z_copy(k, True).wait_recv()
        for source in range(n_row):
            for j in range(2):
                for lane in range(2):
                    zz[lane, pl.ds(source * 2 + j, n_col, stride=8), :] = zbuf[
                        lane, pl.ds(source * 64 + j, n_col, stride=2), :
                    ]
        spread(zz, fin, e_send, e_recv)
        for k in range(1, n_row):
            z_copy(k, False).wait_send()
        collect(zz, fin, e_send, e_recv)
        back = pick(smat[...], jnp.concatenate([fin[0], fin[1]], axis=1))
        basis[step + 1] = back

        @pl.when(step == 0)
        def _():
            vfull[col] = back * SCALE

    @pl.loop(0, ITERS)
    def _(step):
        operate(step)

    u0, b0, b1 = basis[0], basis[1], basis[2]
    over_row(1, [*inner_terms(u0, b1, waves), *inner_terms(b0, b1, waves), square_terms(b1, waves)])
    over_col(1)
    finish_col(0)
    finish_col(1)
    early, late = jnp.sum(gc[0], axis=0), jnp.sum(gc[1], axis=0)
    first, second = krylov_coefficients(
        [early[i : i + 1] for i in range(4)] + [late[i : i + 1] for i in range(5)]
    )
    out_ref[...] = scale_vector(basis[0], first, waves) + scale_vector(basis[1], second, waves)
    for part in range(2):
        for offset in OFFSETS:
            gc_copy(part, offset, False).wait_send()


def on_device(
    rhs, dense, inflow, robin, outflow, trace_row, trace_count, current_row, current_count
):
    n_row = lax.axis_size("row")
    n_col = lax.axis_size("col")
    f32 = jnp.float32
    vmem = pltpu.VMEM
    dma = pltpu.SemaphoreType.DMA
    any_spec = pl.BlockSpec(memory_space=pl.ANY)
    vmem_spec = pl.BlockSpec(memory_space=pltpu.VMEM)
    return pl.pallas_call(
        functools.partial(kernel, n_row, n_col),
        out_shape=jax.ShapeDtypeStruct(rhs.shape, f32),
        in_specs=[any_spec] * 9,
        out_specs=vmem_spec,
        scratch_shapes=[
            vmem((32, 128, 256), f32),
            vmem((32, 512, 256), f32),
            vmem((512, 256), f32),
            vmem((1024, 512), jnp.bfloat16),
            vmem((128, 256), jnp.bfloat16),
            vmem((4, 256, 256), f32),
            vmem((2, 256, 256), f32),
            vmem((2, 128, 256), f32),
            vmem((2, 128, 256), f32),
            vmem((1, 256, 256), f32),
            vmem((1, 256, 256), f32),
            vmem((2, 512, 512), f32),
            vmem((2, 512, 1024), f32),
            vmem((2, 256, 1024), f32),
            vmem((2, 512, 512), f32),
            vmem((2, 256, 1024), f32),
            vmem((2, 256, 1024), f32),
            vmem((256, 512), f32),
            vmem((2, 256, 512), f32),
            vmem((2, 256, 256), f32),
            vmem((2, 256, 256), f32),
            vmem((256, 256), f32),
            vmem((2, 256, 128), f32),
            vmem((2, 256, 128), f32),
            vmem((2, 256, 128), f32),
            vmem((2, 256, 128), f32),
            vmem((3, 128, 256), f32),
            vmem((2, 8, 128), f32),
            vmem((2, 4, 8, 128), f32),
            vmem((2, 8, 128), f32),
            vmem((2, 32, 8, 128), f32),
            vmem((8, 128), jnp.int32), vmem((32, 128), jnp.int32),
            vmem((2, 128), jnp.int32), vmem((128, 128), jnp.int32),
            dma((18,)), dma((2, 32)), dma((62,)), dma((32, 2)), dma((6,)), dma((6,)),
            dma((32,)), dma((32,)), dma((2,)), dma((2,)), dma((2,)), dma((2,)), dma((4,)), dma((4,)),
            dma((32,)), dma((32,)), dma((2, 4)), dma((2, 4)), dma((2, 32)), dma((2, 32)),
        ],
        compiler_params=pltpu.CompilerParams(
            collective_id=0, has_side_effects=True, vmem_limit_bytes=62 * 1024 * 1024
        ),
        name="gmres",
    )(
        rhs, dense, inflow, robin, outflow,
        trace_row.transpose(0, 2, 1), trace_count, current_row.transpose(0, 2, 1), current_count,
    )


def solution(mesh):
    placed = (
        P(("row", "col"), None),
        P(None, "col", "row"),
        P(("row", "col"), None, None, None, None),
        P(("row", "col"), None, None, None, None),
        P(("row", "col"), None, None, None),
        P(),
        P(),
        P(),
        P(),
    )
    return jax.shard_map(
        on_device, mesh=mesh, in_specs=placed, out_specs=P(("row", "col"), None), check_vma=False
    )
```
